32 devices in a mesh: seq: 16 (over z, x, core), dp: 2 (over y).
Axes of the slice: x: 2, y: 2, z: 4, core: 2. Of those that a mesh axis runs over, the one named last changes fastest.
Arguments:
- inputs: bfloat16 [2, 2048, 2048], P('dp', 'seq'), may hold values from -6 to 6
- step_sizes: float32 [2, 2048, 32], P('dp', 'seq'), may hold values from 0.5 to 2
- write_vecs: bfloat16 [2, 2048, 64], P('dp', 'seq'), may hold values from -0.29882812 to 0.29882812
- read_vecs: bfloat16 [2, 2048, 64], P('dp', 'seq'), may hold values from -0.29882812 to 0.29882812
- log_rates: float32 [32], replicated, may hold values from -10 to -3.2
- skip_gain: float32 [32], replicated, may hold values from 0.5 to 1.5
- resets: int32 [2, 8], P('dp'), may hold values from 1 to 2047
- cotangent: bfloat16 [2, 2048, 2048], P('dp', 'seq'), may hold values from -3 to 3
Outputs:
- outputs: bfloat16 [2, 2048, 2048], P('dp', 'seq')
- grad_inputs: bfloat16 [2, 2048, 2048], P('dp', 'seq')
- grad_steps: float32 [2, 2048, 32], P('dp', 'seq')
- grad_write: float32 [2, 2048, 64], P('dp', 'seq')
- grad_read: float32 [2, 2048, 64], P('dp', 'seq')
- grad_rates: float32 [32], replicated
- grad_skip: float32 [32], replicated
The draws below stay inside these ranges and needn't reach their ends.
All inputs are finite; a program needn't handle non-finite values.
Results may differ from the reference program's by a relative error of at most 0.0044.
Values sent between devices are 32-bit elements; how exact they have to be, the bound alone decides.
No kernel may reach another device: no remote copies, remote signals or barrier semaphores. Data moves between devices by JAX's collectives and lax.ppermute only.
A program may use at most 256 MiB of HBM per device.

```python
import math
import jax
import jax.numpy as jnp
from jax import lax

OWNED_CHANNELS = 32
HEAD_DIM = 64
STATE_DIM = 64
TOK_DEV = 128
RESETS = 8
HORIZON_LENGTH = 2048
EPISODE_COUNT = 2
N_SEQ = 16
N_DP = 2


def draw_step_sizes(key, part):
    tier_seed, spurt_seed = jax.random.split(jax.random.fold_in(key, 11))
    level = jax.random.uniform(tier_seed, (EPISODE_COUNT, HORIZON_LENGTH, OWNED_CHANNELS), jnp.float32)
    spurt_clusters = jax.random.uniform(spurt_seed, (EPISODE_COUNT, HORIZON_LENGTH, OWNED_CHANNELS), jnp.float32) < 0.01
    payload_matrix = 0.5 * jnp.exp(level * math.log(2.0))
    payload_matrix = jnp.where(spurt_clusters, 2.0, payload_matrix)
    return payload_matrix.astype(jnp.float32)


def draw_resets(key, part):
    key_early, key_late = jax.random.split(jax.random.fold_in(key, 23))
    half_count = RESETS // 2
    early_steps = jax.random.randint(key_early, (EPISODE_COUNT, half_count), 1, TOK_DEV, dtype=jnp.int32)
    late_steps = jax.random.randint(key_late, (EPISODE_COUNT, RESETS - half_count), HORIZON_LENGTH - TOK_DEV, HORIZON_LENGTH, dtype=jnp.int32)
    early_steps = early_steps.at[:, 0].set(1)
    late_steps = late_steps.at[:, -1].set(HORIZON_LENGTH - 1)
    return jnp.concatenate([early_steps, late_steps], axis=1).astype(jnp.int32)


def shard_levels(stream_key, extent, cuts, smallest, top_value):
    factor_of = 1.0
    for dim, blocks in cuts:
        steps = jax.random.uniform(jax.random.fold_in(jax.random.fold_in(stream_key, 6), dim), (blocks,), jnp.float32, smallest / len(cuts), top_value / len(cuts))
        factor_of = factor_of * jnp.repeat(jnp.exp(steps), extent[dim] // blocks).reshape((-1,) + (1,) * (len(extent) - 1 - dim))
    return factor_of


def centred(own_key, extent, spread, limit, cuts=(), kind=jnp.bfloat16):
    loudness = shard_levels(own_key, extent, cuts, -0.22, 0.18) if cuts else 1.0
    entries = jax.random.normal(own_key, extent, jnp.float32) * spread * loudness
    return jnp.minimum(jnp.maximum(entries, -limit), limit).astype(kind)


def setup_inputs(seed: int = 0) -> dict:
    key_list = jax.random.split(jax.random.key(seed), 9)
    return {
        "inputs": centred(key_list[0], (EPISODE_COUNT, HORIZON_LENGTH, OWNED_CHANNELS * HEAD_DIM), 1.0, 6.0, ((0, 2), (1, 16))),
        "step_sizes": draw_step_sizes(jax.random.fold_in(key_list[8], 71), 0),
        "write_vecs": centred(key_list[2], (EPISODE_COUNT, HORIZON_LENGTH, STATE_DIM), 0.05, 0.29882812, ((0, 2), (1, 16))),
        "read_vecs": centred(key_list[3], (EPISODE_COUNT, HORIZON_LENGTH, STATE_DIM), 0.05, 0.29882812, ((0, 2), (1, 16))),
        "log_rates": jnp.clip(jax.random.uniform(key_list[4], (OWNED_CHANNELS,), jnp.float32, -10.0, -3.2), -10.0, -3.2),
        "skip_gain": jnp.clip(jax.random.uniform(key_list[5], (OWNED_CHANNELS,), jnp.float32, 0.5, 1.5), 0.5, 1.5),
        "resets": draw_resets(jax.random.fold_in(key_list[8], 71), 0),
        "cotangent": centred(key_list[7], (EPISODE_COUNT, HORIZON_LENGTH, OWNED_CHANNELS * HEAD_DIM), 0.5, 3.0, ((0, 2), (1, 16))),
    }


HIGHEST = lax.Precision.HIGHEST


def block_local(log_step, cutoff, write_mat, read_mat, scaled, grad_out):
    length, head_count = log_step.shape
    head_width = scaled.shape[2]
    group_size = min(8, head_count)
    group_count = head_count // group_size
    cumlog = jnp.cumsum(log_step, axis=0)
    segment = jnp.cumsum(cutoff)
    places = jnp.arange(length)
    causal = (places[:, None] >= places[None, :]) & (segment[:, None] == segment[None, :])
    scores = jnp.dot(read_mat, write_mat.T, preferred_element_type=jnp.float32)

    def per_group(operands):
        cum_part, scaled_part, grad_part = operands
        span_log = cum_part[:, :, None] - cum_part[:, None, :]
        decays = jnp.where(causal[None], jnp.exp(jnp.where(causal[None], span_log, 0.0)), 0.0)
        weights = (scores[None] * decays).astype(jnp.bfloat16).astype(jnp.float32)
        scaled_full = scaled_part.astype(jnp.float32)
        grad_full = grad_part.astype(jnp.float32)
        out_part = jnp.einsum("gts,sgp->tgp", weights, scaled_full, precision=HIGHEST)
        back_part = jnp.einsum("gts,tgp->sgp", weights, grad_full, precision=HIGHEST)
        pair_dot = jnp.einsum("tgp,sgp->gts", grad_full, scaled_full, precision=HIGHEST)
        weighted = decays * pair_dot
        kernel = scores[None] * weighted
        return out_part, back_part, jnp.sum(weighted, axis=0), jnp.sum(kernel, axis=2) - jnp.sum(kernel, axis=1)

    cum_groups = cumlog.T.reshape(group_count, group_size, length)
    scaled_groups = scaled.reshape(length, group_count, group_size, head_width).transpose(1, 0, 2, 3)
    grad_groups = grad_out.reshape(length, group_count, group_size, head_width).transpose(1, 0, 2, 3)
    out_all, back_all, weighted_all, dcum_all = lax.map(per_group, (cum_groups, scaled_groups, grad_groups))
    intra_out = out_all.transpose(1, 0, 2, 3).reshape(length, head_count, head_width)
    intra_back = back_all.transpose(1, 0, 2, 3).reshape(length, head_count, head_width)
    weighted_sum = jnp.sum(weighted_all, axis=0)
    dcum = dcum_all.reshape(head_count, length).T
    local_grad = jnp.flip(jnp.cumsum(jnp.flip(dcum, 0), axis=0), 0)
    to_end = jnp.exp(cumlog[-1][None, :] - cumlog) * (segment[-1] == segment).astype(jnp.float32)[:, None]
    from_start = jnp.exp(cumlog) * (segment == 0).astype(jnp.float32)[:, None]
    chain_total = jnp.exp(cumlog[-1]) * (segment[-1] == 0).astype(jnp.float32)
    end_scaled = to_end[:, :, None] * scaled.astype(jnp.float32)
    start_grad = from_start[:, :, None] * grad_out.astype(jnp.float32)
    write_full = write_mat.astype(jnp.float32)
    read_full = read_mat.astype(jnp.float32)
    carry_state = jnp.einsum("sn,shp->hnp", write_full, end_scaled, precision=HIGHEST)
    adjoint_state = jnp.einsum("tn,thp->hnp", read_full, start_grad, precision=HIGHEST)
    return (intra_out, intra_back, local_grad, weighted_sum, chain_total, from_start, to_end, end_scaled, start_grad, carry_state, adjoint_state)


def block_finish(pieces, scaled, grad_out, write_mat, read_mat, carry_in, adjoint_in):
    intra_out, intra_back, local_grad, weighted_sum, chain_total, from_start, to_end, end_scaled, start_grad = pieces[:9]
    write_full = write_mat.astype(jnp.float32)
    read_full = read_mat.astype(jnp.float32)
    across_out = from_start[:, :, None] * jnp.einsum("tn,hnp->thp", read_full, carry_in, precision=HIGHEST)
    across_back = to_end[:, :, None] * jnp.einsum("sn,hnp->shp", write_full, adjoint_in, precision=HIGHEST)
    grad_read = jnp.dot(weighted_sum, write_full, precision=HIGHEST) + jnp.einsum("hnp,thp->tn", carry_in, start_grad, precision=HIGHEST)
    grad_write = jnp.dot(weighted_sum.T, read_full, precision=HIGHEST) + jnp.einsum("hnp,shp->sn", adjoint_in, end_scaled, precision=HIGHEST)
    inflow = jnp.sum(across_out * grad_out.astype(jnp.float32), axis=2)
    outflow = jnp.sum(across_back * scaled.astype(jnp.float32), axis=2)
    log_grads = local_grad + jnp.flip(jnp.cumsum(jnp.flip(inflow, 0), axis=0), 0) + jnp.cumsum(outflow, axis=0) - outflow
    log_grads = log_grads + chain_total[None, :] * jnp.sum(carry_in * adjoint_in, axis=(1, 2))[None, :]
    return intra_out + across_out, intra_back + across_back, grad_read, grad_write, log_grads


def direction(log_step, cutoff, write_mat, read_mat, scaled, grad_out):
    def to_blocks(array):
        return array.reshape((N_SEQ, TOK_DEV) + array.shape[1:])

    operands = tuple(to_blocks(a) for a in (log_step, cutoff, write_mat, read_mat, scaled, grad_out))
    pieces = lax.map(lambda o: block_local(o[0], o[1], o[2], o[3], o[4], o[5]), operands)
    totals, carries, adjoints = pieces[4], pieces[9], pieces[10]

    def rise(running, element):
        return element[0][:, None, None] * running + element[1], running

    empty = jnp.zeros_like(carries[0])
    _, carry_in = lax.scan(rise, empty, (totals, carries))
    _, adjoint_in = lax.scan(rise, empty, (totals, adjoints), reverse=True)
    results = lax.map(lambda o: block_finish(o[0], o[1], o[2], o[3], o[4], o[5], o[6]), (pieces, operands[4], operands[5], operands[2], operands[3], carry_in, adjoint_in))
    return tuple(r.reshape((HORIZON_LENGTH,) + r.shape[2:]) for r in results)


def reference(inputs, step_sizes, write_vecs, read_vecs, log_rates, skip_gain, resets, cotangent):
    decay_rates = jnp.exp(log_rates)
    places = jnp.arange(HORIZON_LENGTH, dtype=jnp.int32)
    collected = [[], [], [], [], []]
    rate_total = jnp.zeros((OWNED_CHANNELS,), jnp.float32)
    skip_total = jnp.zeros((OWNED_CHANNELS,), jnp.float32)
    for trajectory in range(N_DP):
        features = inputs[trajectory].reshape(HORIZON_LENGTH, OWNED_CHANNELS, HEAD_DIM)
        grad_out = cotangent[trajectory].reshape(HORIZON_LENGTH, OWNED_CHANNELS, HEAD_DIM)
        deltas = step_sizes[trajectory]
        write_mat = write_vecs[trajectory]
        read_mat = read_vecs[trajectory]
        scaled = (deltas[:, :, None] * features).astype(jnp.bfloat16)
        log_step = -deltas * decay_rates[None, :]
        reset_marks = resets[trajectory]
        cut_here = jnp.any(places[:, None] == reset_marks[None, :], axis=1).astype(jnp.float32)
        cut_next = jnp.any(places[:, None] + 1 == reset_marks[None, :], axis=1).astype(jnp.float32)
        fwd_mixed, fwd_back, fwd_read, fwd_write, fwd_log = direction(log_step, cut_here, write_mat, read_mat, scaled, grad_out)
        flipped = tuple(jnp.flip(a, 0) for a in (log_step, cut_next, write_mat, read_mat, scaled, grad_out))
        rev_results = direction(flipped[0], flipped[1], flipped[2], flipped[3], flipped[4], flipped[5])
        rev_mixed, rev_back, rev_read, rev_write, rev_log = tuple(jnp.flip(a, 0) for a in rev_results)
        grad_scaled = fwd_back + rev_back
        log_total = fwd_log + rev_log
        mixed = fwd_mixed + rev_mixed + skip_gain[None, :, None] * features
        collected[0].append(mixed.astype(jnp.bfloat16).reshape(HORIZON_LENGTH, OWNED_CHANNELS * HEAD_DIM))
        grad_in = deltas[:, :, None] * grad_scaled + skip_gain[None, :, None] * grad_out
        collected[1].append(grad_in.astype(jnp.bfloat16).reshape(HORIZON_LENGTH, OWNED_CHANNELS * HEAD_DIM))
        collected[2].append(jnp.sum(features.astype(jnp.float32) * grad_scaled, axis=2) - decay_rates[None, :] * log_total)
        collected[3].append(fwd_write + rev_write)
        collected[4].append(fwd_read + rev_read)
        rate_total = rate_total - jnp.sum(decay_rates[None, :] * deltas * log_total, axis=0)
        skip_total = skip_total + jnp.sum(features.astype(jnp.float32) * grad_out.astype(jnp.float32), axis=(0, 2))
    stacked = [jnp.stack(c, axis=0) for c in collected]
    return (stacked[0], stacked[1], stacked[2], stacked[3], stacked[4], rate_total, skip_total)
```

```python
import functools
import math

import jax
import jax.numpy as jnp
from jax import lax
from jax.experimental import pallas as pl
from jax.experimental.pallas import tpu as pltpu
from jax.sharding import PartitionSpec as P

F32 = jnp.float32
BF16 = jnp.bfloat16
LANES = 128
WIDE = 256
CHUNKS = 4
NN = (((1,), (0,)), ((), ()))
NT = (((1,), (1,)), ((), ()))
TN = (((0,), (0,)), ((), ()))


def mm(a, b, dims=NN):
    return lax.dot_general(a, b, dims, preferred_element_type=F32)


def exact(a, b):
    return jnp.dot(a, b, precision=lax.Precision.HIGHEST, preferred_element_type=F32)


def halves(value):
    upper = value.astype(BF16)
    return upper, (value - upper.astype(F32)).astype(BF16)


def thirds(value):
    upper = value.astype(BF16)
    rest = value - upper.astype(F32)
    middle = rest.astype(BF16)
    return upper, middle, (rest - middle.astype(F32)).astype(BF16)


def iota(shape, dim):
    return lax.broadcasted_iota(jnp.int32, shape, dim)


def block_tables(deltas, log_rates, resets_ref, first):
    length = deltas.shape[0]
    square = (length, length)
    row, col = iota(square, 0), iota(square, 1)
    lower = (row >= col).astype(F32)
    upper = (row <= col).astype(F32)
    rates = jnp.exp(log_rates)
    lam = -deltas * rates
    cum = exact(lower, lam)

    def marks(grid, ahead):
        hit = jnp.zeros(square, jnp.bool_)
        for k in range(resets_ref.shape[1]):
            hit = hit | (grid + (first + ahead) == resets_ref[0, k])
        return hit.astype(BF16)

    low16, up16 = lower.astype(BF16), upper.astype(BF16)
    seg_f = mm(low16, marks(row, 0)), mm(marks(col, 0), up16)
    seg_r = mm(up16, marks(row, 1)), mm(marks(col, 1), low16)
    return rates, lam, cum, lower, upper, seg_f, seg_r


def expander(heads, width, start):
    shape = (3 * heads, width)
    per_head = 2 * LANES // 4
    return (iota(shape, 0) % heads == (iota(shape, 1) + start) // per_head).astype(BF16)


def spread_parts(values):
    return jnp.concatenate([jnp.concatenate(thirds(v), axis=1) for v in values], axis=0)


def factors(deltas, lam, cum):
    before = cum - lam
    return [deltas, jnp.exp(cum), jnp.exp(-cum), jnp.exp(-before), jnp.exp(before)]


def place_of(start, parts, chips):
    part, chip = divmod(start // WIDE, chips)
    return part // parts, part % parts, chip


def totals_kernel(deltas_ref, rates_ref, resets_ref, out_ref):
    deltas = deltas_ref[...]
    length, heads = deltas.shape
    first = lax.axis_index("seq") * length
    chain = jnp.exp(-jnp.exp(rates_ref[...]) * jnp.sum(deltas, axis=0, keepdims=True))
    clear_f, clear_r = jnp.float32(1.0), jnp.float32(1.0)
    for k in range(resets_ref.shape[1]):
        at = resets_ref[0, k] - first
        clear_f = jnp.where((at >= 0) & (at < length), 0.0, clear_f)
        clear_r = jnp.where((at >= 1) & (at < length + 1), 0.0, clear_r)
    out_ref[0:1, 0:heads] = chain * clear_f
    out_ref[0:1, heads : 2 * heads] = chain * clear_r


def states_kernel(chunks, chips, x_ref, cot_ref, deltas_ref, write_ref, read_ref, rates_ref, resets_ref, *outs):
    length, channels = x_ref.shape
    heads = deltas_ref.shape[1]
    index = lax.axis_index("seq")
    core = lax.rem(index, 2)
    deltas = deltas_ref[...]
    rates, lam, cum, lower, upper, seg_f, seg_r = block_tables(deltas, rates_ref[...], resets_ref, index * length)
    states = write_ref.shape[1]
    seg_fc, seg_rc = seg_f[0][:, :states], seg_r[0][:, :states]
    write, read = write_ref[...], read_ref[...]
    zero = jnp.zeros_like(write)
    write_f = jnp.where(seg_fc == seg_fc[length - 1 : length], write, zero)
    write_r = jnp.where(seg_rc == seg_rc[0:1], write, zero)
    read_f = jnp.where(seg_fc == 0.0, read, zero)
    read_r = jnp.where(seg_rc == 0.0, read, zero)
    parts = spread_parts(factors(deltas, lam, cum))
    keep, send = outs[:chunks], outs[chunks:]
    for start in range(0, channels, WIDE):
        spread = mm(parts, expander(heads, WIDE, start))
        step, u_f, v_f, u_r, v_r = (spread[i * length : (i + 1) * length] for i in range(5))
        lanes = slice(start, start + WIDE)
        scaled = (step * x_ref[:, lanes].astype(F32)).astype(BF16).astype(F32)
        cot = cot_ref[:, lanes].astype(F32)
        chain = u_f[length - 1 : length]
        carry_f = mm(write_f, (v_f * scaled).astype(BF16), TN) * chain
        carry_r = mm(write_r, (v_r * scaled).astype(BF16), TN)
        adj_f = mm(read_f, (u_f * cot).astype(BF16), TN)
        adj_r = mm(read_r, (u_r * cot).astype(BF16), TN) * chain
        chunk, part, chip = place_of(start, keep[0].shape[2], chips)
        for scan, value in enumerate((carry_f, adj_r, adj_f, carry_r)):
            zeroth, other = value[:, :LANES], value[:, LANES:]
            keep[chunk][scan, chip, part] = jnp.where(core == 0, zeroth, other)
            send[chunk][scan, chip, part] = jnp.where(core == 0, other, zeroth)


class Chain:
    def __init__(self, table_ref, heads, index, chips):
        self.table, self.heads, self.index, self.chips = table_ref, heads, index, chips

    def block(self, device, scan, pair):
        row = jnp.bitwise_xor(self.index, device)
        base = (scan % 2) * self.heads + 2 * pair
        return self.table[row, base], self.table[row, base + 1]

    def over(self, first, count, scan, pair):
        low, high = jnp.float32(1.0), jnp.float32(1.0)
        for k in range(count):
            a, b = self.block(first + k, scan, pair)
            low, high = low * a, high * b
        return low, high


def lanes_of(pair):
    lane = iota((1, LANES), 1)
    return jnp.where(lane < LANES // 2, pair[0], pair[1])


def mul2(a, b):
    return a[0] * b[0], a[1] * b[1]


def pick2(cond, a, b):
    return jnp.where(cond, a[0], b[0]), jnp.where(cond, a[1], b[1])


ONE2 = (1.0, 1.0)


def position(chips):
    index = lax.axis_index("seq")
    core = lax.rem(index, 2)
    chip = lax.rem(lax.div(index, 2), chips)
    return index, core, chip


def pair_number(part, chips, chip, core):
    return (part * chips + chip) * 2 + core


def chip_kernel(chunk, chips, heads, table_ref, keep_ref, got_ref, *outs):
    index, core, chip = position(chips)
    base = index - core
    chain = Chain(table_ref, heads, index, chips)
    parts = keep_ref.shape[2]
    for shift in range(chips):
        owner = lax.rem(chip + shift, chips)
        for part in range(parts):
            pair = pair_number(chunk * parts + part, chips, owner, core)
            for scan in range(4):
                mine, other = keep_ref[scan, owner, part], got_ref[scan, owner, part]
                if scan < 2:
                    factor = chain.block(base + 1, scan, pair)
                    a, b = pick2(core == 0, factor, ONE2), pick2(core == 0, ONE2, factor)
                else:
                    factor = chain.block(base, scan, pair)
                    a, b = pick2(core == 0, ONE2, factor), pick2(core == 0, factor, ONE2)
                outs[shift][scan, part] = lanes_of(a) * mine + lanes_of(b) * other


def plane_kernel(chunk, chips, heads, table_ref, *refs):
    gathered, (out_ref,) = refs[:chips], refs[chips:]
    index, core, chip = position(chips)
    base = index - core - 2 * chip
    chain = Chain(table_ref, heads, index, chips)
    parts = out_ref.shape[1]
    for part in range(parts):
        pair = pair_number(chunk * parts + part, chips, chip, core)
        for scan in range(4):
            whole = [chain.over(base + 2 * other, 2, scan, pair) for other in range(chips)]
            total = None
            for shift in range(chips):
                place = lax.rem(chip + shift, chips)
                weight = ONE2
                for other in range(chips):
                    beyond = other > place if scan < 2 else other < place
                    weight = mul2(weight, pick2(beyond, whole[other], ONE2))
                term = lanes_of(weight) * gathered[shift][scan, part]
                total = term if total is None else total + term
            out_ref[scan, part] = total


def joined(level, chips, chain, plane, scan, pair, entered, got):
    bit = lax.rem(lax.shift_right_logical(plane, level), 2)
    first = plane - lax.rem(plane, 2**level)
    takes = bit == 1 if scan < 2 else bit == 0
    weight = pick2(takes, ONE2, (0.0, 0.0))
    if level > 0:
        for k in range(2**level):
            between = first + k < plane if scan < 2 else first + k > plane
            weight = mul2(weight, pick2(between, chain.over((first + k) * 2 * chips, 2 * chips, scan, pair), ONE2))
    value = lanes_of(weight) * got
    return value if entered is None else entered + value


def hop_kernel(chunk, chips, heads, level, last, table_ref, *refs):
    (entered_ref, refs) = (refs[0], refs[1:]) if level > 0 else (None, refs)
    total_ref, got_ref, new_ref, onward_ref = refs
    index, core, chip = position(chips)
    plane = lax.div(index, 2 * chips)
    chain = Chain(table_ref, heads, index, chips)
    parts = got_ref.shape[1]
    size = 2**level
    bit = lax.rem(lax.shift_right_logical(plane, level), 2)
    after = lax.rem(lax.shift_right_logical(plane, level + 1), 2)
    mine = plane - lax.rem(plane, size)
    far = jnp.bitwise_xor(mine, size)
    for part in range(parts):
        pair = pair_number(chunk * parts + part, chips, chip, core)
        totals = []
        for scan in range(4):
            got, own = got_ref[scan, part], total_ref[scan, part]
            entered = entered_ref[scan, part] if level > 0 else None
            new_ref[scan, part] = joined(level, chips, chain, plane, scan, pair, entered, got)
            near_factor = chain.over(mine * 2 * chips, 2 * chips * size, scan, pair)
            far_factor = chain.over(far * 2 * chips, 2 * chips * size, scan, pair)
            later = bit == 1 if scan < 2 else bit == 0
            a, b = pick2(later, ONE2, far_factor), pick2(later, near_factor, ONE2)
            totals.append(lanes_of(a) * own + lanes_of(b) * got)
        if last:
            for scan in range(2):
                onward_ref[scan, part] = jnp.where(after == 0, totals[scan], totals[scan + 2])
        else:
            for scan in range(4):
                onward_ref[scan, part] = totals[scan]


def spread_kernel(chunk, chips, heads, level, table_ref, entered_ref, got_ref, *refs):
    gathered, outs = refs[:chips], refs[chips:]
    index, core, chip = position(chips)
    plane = lax.div(index, 2 * chips)
    chain = Chain(table_ref, heads, index, chips)
    parts = got_ref.shape[1]
    base = plane * 2 * chips
    for part in range(parts):
        pair = pair_number(chunk * parts + part, chips, chip, core)
        for scan in range(4):
            value = joined(level, chips, chain, plane, scan, pair, entered_ref[scan, part], got_ref[scan % 2, part])
            whole = [chain.over(base + 2 * other, 2, scan, pair) for other in range(chips)]
            for shift in range(chips):
                target = lax.rem(chip + shift, chips)
                weight = ONE2
                for other in range(chips):
                    ahead = other < target if scan < 2 else other > target
                    weight = mul2(weight, pick2(ahead, whole[other], ONE2))
                total = lanes_of(weight) * value
                for source in range(chips):
                    if source == shift:
                        continue
                    place = lax.rem(chip + source, chips)
                    counts = place < target if scan < 2 else place > target
                    weight = pick2(counts, ONE2, (0.0, 0.0))
                    for other in range(chips if chips > 2 else 0):
                        if scan < 2:
                            between = (other > place) & (other < target)
                        else:
                            between = (other < place) & (other > target)
                        weight = mul2(weight, pick2(between, whole[other], ONE2))
                    total = total + lanes_of(weight) * gathered[source][scan, part]
                outs[shift][scan, part] = total


def core_kernel(chunk, chips, heads, table_ref, keep_ref, got_ref, *refs):
    entered, (own_ref, send_ref) = refs[:chips], refs[chips:]
    index, core, chip = position(chips)
    chain = Chain(table_ref, heads, index, chips)
    parts = keep_ref.shape[2]
    for shift in range(chips):
        owner = lax.rem(chip + chips - shift, chips)
        for part in range(parts):
            pair = pair_number(chunk * parts + part, chips, owner, core)
            for scan in range(4):
                value = entered[shift][scan, part]
                mine, other = keep_ref[scan, owner, part], got_ref[scan, owner, part]
                near = core == 0 if scan < 2 else core == 1
                to_own = lanes_of(chain.block(jnp.bitwise_xor(index, 1), scan, pair)) * value + other
                to_other = lanes_of(chain.block(index, scan, pair)) * value + mine
                own_ref[scan, owner, part] = jnp.where(near, value, to_own)
                send_ref[scan, owner, part] = jnp.where(near, to_other, value)


def finish_kernel(chunks, chips, x_ref, cot_ref, deltas_ref, write_ref, read_ref, rates_ref, skip_ref, resets_ref, *refs):
    own, got = refs[:chunks], refs[chunks : 2 * chunks]
    out_ref, gin_ref, steps_ref, gwrite_ref, gread_ref, small_ref = refs[2 * chunks :]
    length, channels = x_ref.shape
    heads = deltas_ref.shape[1]
    states = write_ref.shape[1]
    index = lax.axis_index("seq")
    core = lax.rem(index, 2)
    deltas = deltas_ref[...]
    rates, lam, cum, lower, upper, seg_f, seg_r = block_tables(deltas, rates_ref[...], resets_ref, index * length)
    mask_f = (lower > 0.0) & (seg_f[0] == seg_f[1])
    mask_r = (upper > 0.0) & (seg_r[0] == seg_r[1])
    seg_fc, seg_rc = seg_f[0][:, :states], seg_r[0][:, :states]
    end_f, end_r = seg_fc == seg_fc[length - 1 : length], seg_rc == seg_rc[0:1]
    start_f, start_r = seg_fc == 0.0, seg_rc == 0.0
    write, read = write_ref[...], read_ref[...]
    zero = jnp.zeros_like(write)
    write_f, write_r = jnp.where(end_f, write, zero), jnp.where(end_r, write, zero)
    read_f, read_r = jnp.where(start_f, read, zero), jnp.where(start_r, read, zero)
    scores = mm(read, write, NT)
    scores_f = jnp.where(mask_f, scores, 0.0).astype(BF16)
    scores_r = jnp.where(mask_r, scores, 0.0).astype(BF16)
    open_f = jnp.where(seg_f[0][length - 1 : length, 0:1] == 0.0, 1.0, 0.0)
    open_r = jnp.where(seg_r[0][0:1, 0:1] == 0.0, 1.0, 0.0)
    skip = jnp.broadcast_to(skip_ref[...], (8, heads))
    parts = spread_parts(factors(deltas, lam, cum) + [skip])
    flow_f = jnp.zeros((length, heads), F32)
    flow_r = jnp.zeros((length, heads), F32)
    direct = jnp.zeros((length, heads), F32)
    rows = jnp.zeros((8, heads), F32)
    pair_f = jnp.zeros((length, length), F32)
    pair_r = jnp.zeros((length, length), F32)
    acc_read_f = jnp.zeros((length, states), F32)
    acc_read_r = jnp.zeros((length, states), F32)
    acc_write_f = jnp.zeros((length, states), F32)
    acc_write_r = jnp.zeros((length, states), F32)
    for start in range(0, channels, WIDE):
        expand = expander(heads, WIDE, start)
        spread = mm(parts, expand)
        step, u_f, v_f, u_r, v_r = (spread[i * length : (i + 1) * length] for i in range(5))
        gain = spread[5 * length : 5 * length + 1]
        lanes = slice(start, start + WIDE)
        x = x_ref[:, lanes].astype(F32)
        cot = cot_ref[:, lanes].astype(F32)
        scaled = (step * x).astype(BF16).astype(F32)
        chain = u_f[length - 1 : length]
        sc_f, sc_r = (v_f * scaled).astype(BF16), (v_r * scaled).astype(BF16)
        ct_f, ct_r = (u_f * cot).astype(BF16), (u_r * cot).astype(BF16)
        chunk, part, chip = place_of(start, own[0].shape[2], chips)
        entering = []
        for scan in range(4):
            a, b = own[chunk][scan, chip, part], got[chunk][scan, chip, part]
            entering.append(jnp.concatenate([jnp.where(core == 0, a, b), jnp.where(core == 0, b, a)], axis=1))
        in_f, back_r, back_f, in_r = entering
        in_f16, in_r16 = in_f.astype(BF16), (in_r * chain).astype(BF16)
        back_f16, back_r16 = (back_f * chain).astype(BF16), back_r.astype(BF16)
        y_f = u_f * (mm(scores_f, sc_f) + mm(read_f, in_f16))
        y_r = u_r * (mm(scores_r, sc_r) + mm(read_r, in_r16))
        g_f = v_f * (mm(scores_f, ct_f, TN) + mm(write_f, back_f16))
        g_r = v_r * (mm(scores_r, ct_r, TN) + mm(write_r, back_r16))
        out_ref[:, lanes] = (y_f + y_r + gain * x).astype(BF16)
        grad = g_f + g_r
        gin_ref[:, lanes] = (step * grad + gain * cot).astype(BF16)
        local_f, local_r = mm(write_f, sc_f, TN) * chain, mm(write_r, sc_r, TN)
        through = back_f * (local_f + open_f * chain * in_f) + back_r * (local_r + open_r * chain * in_r)
        through = jnp.sum(through, axis=0, keepdims=True)
        own_skip = jnp.sum(x * cot, axis=0, keepdims=True)
        small = jnp.concatenate([through, own_skip, jnp.zeros((6, WIDE), F32)], axis=0)
        flows = jnp.concatenate([cot * y_f - scaled * g_f, cot * y_r - scaled * g_r, x * grad, small], axis=0)
        high, low = halves(flows)
        collect = expand[:heads]
        sums = mm(high, collect, NT) + mm(low, collect, NT)
        flow_f = flow_f + sums[:length]
        flow_r = flow_r + sums[length : 2 * length]
        direct = direct + sums[2 * length : 3 * length]
        rows = rows + sums[3 * length :]
        pair_f = pair_f + mm(ct_f, sc_f, NT)
        pair_r = pair_r + mm(ct_r, sc_r, NT)
        acc_read_f = acc_read_f + mm(ct_f, in_f16, NT)
        acc_read_r = acc_read_r + mm(ct_r, in_r16, NT)
        acc_write_f = acc_write_f + mm(sc_f, back_f16, NT)
        acc_write_r = acc_write_r + mm(sc_r, back_r16, NT)
    pairs = (jnp.where(mask_f, pair_f, 0.0) + jnp.where(mask_r, pair_r, 0.0)).astype(BF16)
    gread_ref[...] = mm(pairs, write) + jnp.where(start_f, acc_read_f, 0.0) + jnp.where(start_r, acc_read_r, 0.0)
    gwrite_ref[...] = mm(pairs, read, TN) + jnp.where(end_f, acc_write_f, 0.0) + jnp.where(end_r, acc_write_r, 0.0)
    logs = exact(upper, flow_f) + exact(lower, flow_r) + rows[0:1]
    steps_ref[...] = direct - rates * logs
    small_ref[0:1] = -rates * jnp.sum(deltas * logs, axis=0, keepdims=True)
    small_ref[1:2] = rows[1:2]


def call(body, out_shape, scalars, count, flops, size, name):
    in_specs = [pl.BlockSpec(memory_space=pltpu.SMEM if i in scalars else pltpu.VMEM) for i in range(count)]
    return pl.pallas_call(
        body,
        out_shape=out_shape,
        in_specs=in_specs,
        out_specs=jax.tree.map(lambda _: pl.BlockSpec(memory_space=pltpu.VMEM), out_shape),
        compiler_params=pltpu.CompilerParams(vmem_limit_bytes=40 << 20),
        cost_estimate=pl.CostEstimate(flops=flops, bytes_accessed=size, transcendentals=0),
        name=name,
    )


def local(chips, inputs, step_sizes, write_vecs, read_vecs, log_rates, skip_gain, resets, cotangent):
    x, deltas, write, read, cot = inputs[0], step_sizes[0], write_vecs[0], read_vecs[0], cotangent[0]
    length, channels = x.shape
    heads, states = deltas.shape[1], write.shape[1]
    devices = lax.axis_size("seq")
    planes = devices // (2 * chips)
    levels = int(math.log2(planes))
    chunks = min(CHUNKS, channels // (WIDE * chips))
    parts = channels // (WIDE * chips * chunks)
    rates, skip = log_rates[None], skip_gain[None]

    def like(*shape, kind=F32):
        return jax.ShapeDtypeStruct(shape, kind)

    table = call(totals_kernel, like(1, 2 * heads), (2,), 3, 10000, 20000, "totals")(deltas, rates, resets)
    reach = 1
    while reach < devices:
        far = lax.ppermute(table, "seq", [(i, i ^ reach) for i in range(devices)])
        table = jnp.concatenate([table, far], axis=0)
        reach *= 2

    group = like(4, chips, parts, states, LANES)
    single = like(4, parts, states, LANES)
    half = like(2, parts, states, LANES)
    made = call(functools.partial(states_kernel, chunks, chips), [group] * (2 * chunks), (6,), 7, 300 * 10**6, 4 * 10**6, "states")(
        x, cot, deltas, write, read, rates, resets
    )
    keep, send = made[:chunks], made[chunks:]

    def device(plane, chip, core):
        return (plane * chips + chip) * 2 + core

    every = [(p, a, c) for p in range(planes) for a in range(chips) for c in range(2)]
    swap = [(device(p, a, c), device(p, a, 1 - c)) for p, a, c in every]

    def turn(shift):
        return [(device(p, a, c), device(p, (a + shift) % chips, c)) for p, a, c in every]

    def across(level):
        return [(device(p, a, c), device(p ^ 2**level, a, c)) for p, a, c in every]

    def send_to(value, perm):
        return lax.ppermute(value, "seq", perm)

    size = 4 * parts * states * LANES * 4
    owns, gots = [], []
    for k in range(chunks):
        got = send_to(send[k], swap)
        chip_totals = call(functools.partial(chip_kernel, k, chips, heads), [single] * chips, (0,), 3, 10**6, size * 6, "chip")(
            table, keep[k], got
        )
        gathered = [chip_totals[0]] + [None] * (chips - 1)
        for shift in range(1, chips):
            gathered[chips - shift] = send_to(chip_totals[shift], turn(shift))
        (onward,) = call(functools.partial(plane_kernel, k, chips, heads), [single], (0,), 1 + chips, 10**6, size * 3, "plane")(table, *gathered)
        before = []
        for level in range(levels - 1):
            arrived = send_to(onward, across(level))
            last = level == levels - 2
            hop = call(
                functools.partial(hop_kernel, k, chips, heads, level, last),
                [single, half if last else single],
                (0,),
                3 + len(before),
                10**6,
                size * 4,
                "hop",
            )
            entry, onward = hop(table, *before, onward, arrived)
            before = [entry]
        arrived = send_to(onward, across(levels - 1))
        placed = call(
            functools.partial(spread_kernel, k, chips, heads, levels - 1), [single] * chips, (0,), 3 + chips, 10**6, size * 5, "spread"
        )(table, *before, arrived, *gathered)
        entered = [placed[0]] + [send_to(placed[shift], turn(shift)) for shift in range(1, chips)]
        mine, theirs = call(functools.partial(core_kernel, k, chips, heads), [group] * 2, (0,), 3 + chips, 10**6, size * 8, "core")(
            table, keep[k], got, *entered
        )
        owns.append(mine)
        gots.append(send_to(theirs, swap))

    outputs, grad_inputs, grad_steps, grad_write, grad_read, small = call(
        functools.partial(finish_kernel, chunks, chips),
        [
            like(length, channels, kind=BF16),
            like(length, channels, kind=BF16),
            like(length, heads),
            like(length, states),
            like(length, states),
            like(2, heads),
        ],
        (7,),
        8 + 2 * chunks,
        2 * 10**9,
        6 * 10**6,
        "finish",
    )(x, cot, deltas, write, read, rates, skip, resets, *owns, *gots)
    count = devices * lax.axis_size("dp")
    spread = jnp.broadcast_to(small[None], (count,) + small.shape)
    total = jnp.sum(lax.all_to_all(spread, ("seq", "dp"), 0, 0, tiled=True), axis=0)
    return (outputs[None], grad_inputs[None], grad_steps[None], grad_write[None], grad_read[None], total[0], total[1])


def solution(mesh):
    along = P("dp", "seq", None)
    chips = 2 ** (int(math.log2(mesh.shape["seq"] // 2)) // 2)
    return jax.shard_map(
        functools.partial(local, chips),
        mesh=mesh,
        in_specs=(along, along, along, along, P(), P(), P("dp", None), along),
        out_specs=(along, along, along, along, along, P(), P()),
        check_vma=False,
    )
```

```python
import functools
import math

import jax
import jax.numpy as jnp
from jax import lax
from jax.experimental import pallas as pl
from jax.experimental.pallas import tpu as pltpu
from jax.sharding import PartitionSpec as P

F32 = jnp.float32
BF16 = jnp.bfloat16
LANES = 128
WIDE = 256
STATES = 64
RESETS = 8
CHUNKS = 4
ROOM = 16
NN = (((1,), (0,)), ((), ()))
NT = (((1,), (1,)), ((), ()))
TN = (((0,), (0,)), ((), ()))


def mm(a, b, dims=NN):
    return lax.dot_general(a, b, dims, preferred_element_type=F32)


def exact(a, b):
    return jnp.dot(a, b, precision=lax.Precision.HIGHEST, preferred_element_type=F32)


def halves(value):
    upper = value.astype(BF16)
    return upper, (value - upper.astype(F32)).astype(BF16)


def thirds(value):
    upper = value.astype(BF16)
    rest = value - upper.astype(F32)
    middle = rest.astype(BF16)
    return upper, middle, (rest - middle.astype(F32)).astype(BF16)


def iota(shape, dim):
    return lax.broadcasted_iota(jnp.int32, shape, dim)


def block_tables(deltas, log_rates, resets, first):
    length = deltas.shape[0]
    square = (length, length)
    row, col = iota(square, 0), iota(square, 1)
    lower = (row >= col).astype(F32)
    upper = (row <= col).astype(F32)
    rates = jnp.exp(log_rates)
    lam = -deltas * rates
    cum = exact(lower, lam)

    def marks(grid, ahead):
        hit = jnp.zeros(square, jnp.bool_)
        for k in range(RESETS):
            hit = hit | (grid + (first + ahead) == resets[0:1, k : k + 1])
        return hit.astype(BF16)

    low16, up16 = lower.astype(BF16), upper.astype(BF16)
    seg_f = mm(low16, marks(row, 0)), mm(marks(col, 0), up16)
    seg_r = mm(up16, marks(row, 1)), mm(marks(col, 1), low16)
    return rates, lam, cum, lower, upper, seg_f, seg_r


def expander(heads, width, start):
    shape = (3 * heads, width)
    per_head = 2 * LANES // 4
    return (iota(shape, 0) % heads == (iota(shape, 1) + start) // per_head).astype(BF16)


def spread_parts(values):
    return jnp.concatenate([jnp.concatenate(thirds(v), axis=1) for v in values], axis=0)


def factors(deltas, lam, cum):
    before = cum - lam
    return [deltas, jnp.exp(cum), jnp.exp(-cum), jnp.exp(-before), jnp.exp(before)]


def place_of(start, parts, chips):
    part, chip = divmod(start // WIDE, chips)
    return part // parts, part % parts, chip


class Packed:
    def __init__(self, pack_ref, heads, states):
        self.deltas = pack_ref[0:heads].T
        self.write = pack_ref[heads : heads + states].T.astype(BF16)
        self.read = pack_ref[heads + states : heads + 2 * states].T.astype(BF16)
        rows = heads + 2 * states
        self.log_rates = pack_ref[rows : rows + 1, 0:heads]
        self.skip = pack_ref[rows + 1 : rows + 2, 0:heads]
        self.resets = pack_ref[rows + 2 : rows + 3].astype(jnp.int32)


def states_kernel(chunks, chips, heads, states, x_hbm, cot_hbm, pack_ref, *refs):
    outs, (x_ref, cot_ref, wide_sem) = refs[: 2 * chunks], refs[2 * chunks :]
    length, channels = x_ref.shape
    starts = range(0, channels, WIDE)
    wides = [
        [
            pltpu.make_async_copy(source.at[:, pl.ds(start, WIDE)], target.at[:, pl.ds(start, WIDE)], wide_sem.at[i, start // WIDE])
            for i, (source, target) in enumerate(((x_hbm, x_ref), (cot_hbm, cot_ref)))
        ]
        for start in starts
    ]
    for both in wides:
        for copy in both:
            copy.start()
    index = lax.axis_index("seq")
    core = lax.rem(index, 2)
    given = Packed(pack_ref, heads, states)
    deltas = given.deltas
    rates, lam, cum, lower, upper, seg_f, seg_r = block_tables(deltas, given.log_rates, given.resets, index * length)
    seg_fc, seg_rc = seg_f[0][:, :states], seg_r[0][:, :states]
    write, read = given.write, given.read
    zero = jnp.zeros_like(write)
    write_f = jnp.where(seg_fc == seg_fc[length - 1 : length], write, zero)
    write_r = jnp.where(seg_rc == seg_rc[0:1], write, zero)
    read_f = jnp.where(seg_fc == 0.0, read, zero)
    read_r = jnp.where(seg_rc == 0.0, read, zero)
    open_f = jnp.where(seg_f[0][length - 1 : length, 0:1] == 0.0, 1.0, 0.0)
    open_r = jnp.where(seg_r[0][0:1, 0:1] == 0.0, 1.0, 0.0)
    parts = spread_parts(factors(deltas, lam, cum))
    keep, send = outs[:chunks], outs[chunks:]
    for start in starts:
        spread = mm(parts, expander(heads, WIDE, start))
        for copy in wides[start // WIDE]:
            copy.wait()
        step, u_f, v_f, u_r, v_r = (spread[i * length : (i + 1) * length] for i in range(5))
        lanes = slice(start, start + WIDE)
        scaled = (step * x_ref[:, lanes].astype(F32)).astype(BF16).astype(F32)
        cot = cot_ref[:, lanes].astype(F32)
        chain = u_f[length - 1 : length]
        carry_f = mm(write_f, (v_f * scaled).astype(BF16), TN) * chain
        carry_r = mm(write_r, (v_r * scaled).astype(BF16), TN)
        adj_f = mm(read_f, (u_f * cot).astype(BF16), TN)
        adj_r = mm(read_r, (u_r * cot).astype(BF16), TN) * chain
        tail = jnp.concatenate([open_f * chain, open_r * chain, jnp.zeros((6, WIDE), F32)], axis=0)
        chunk, part, chip = place_of(start, keep[0].shape[1], chips)
        rows = 0
        for value in (carry_f, adj_r, adj_f, carry_r, tail):
            zeroth, other = value[:, :LANES], value[:, LANES:]
            span = pl.ds(rows, value.shape[0])
            keep[chunk][chip, part, span] = jnp.where(core == 0, zeroth, other)
            send[chunk][chip, part, span] = jnp.where(core == 0, other, zeroth)
            rows += value.shape[0]


def position(chips):
    index = lax.axis_index("seq")
    core = lax.rem(index, 2)
    chip = lax.rem(lax.div(index, 2), chips)
    return core, chip, lax.div(index, 2 * chips)


def rows_of(scan):
    return pl.ds(scan * STATES, STATES)


def factor_of(ref, at, scan):
    return ref[(*at, pl.ds(4 * STATES + scan % 2, 1))]


def put_factors(ref, at, forward, reverse):
    ref[(*at, pl.ds(4 * STATES, 8))] = jnp.concatenate([forward, reverse, jnp.zeros((6, LANES), F32)], axis=0)


def chip_kernel(chips, keep_ref, got_ref, *outs):
    core, chip, _ = position(chips)
    for shift in range(chips):
        owner = lax.rem(chip + shift, chips)
        for part in range(keep_ref.shape[1]):
            at = (owner, part)
            for scan in range(4):
                mine, other = keep_ref[(*at, rows_of(scan))], got_ref[(*at, rows_of(scan))]
                own, far = factor_of(keep_ref, at, scan), factor_of(got_ref, at, scan)
                later = core == 1 if scan < 2 else core == 0
                outs[shift][part, rows_of(scan)] = jnp.where(later, mine + own * other, other + far * mine)
            both = [factor_of(keep_ref, at, scan) * factor_of(got_ref, at, scan) for scan in range(2)]
            put_factors(outs[shift], (part,), *both)


def plane_kernel(chips, _, *refs):
    gathered, out_ref = refs[:chips], refs[chips]
    _, chip, _ = position(chips)
    places = [lax.rem(chip + shift, chips) for shift in range(chips)]
    for part in range(out_ref.shape[0]):
        for scan in range(4):
            total = None
            for shift in range(chips):
                term = gathered[shift][part, rows_of(scan)]
                for other in range(chips):
                    if other != shift:
                        beyond = places[other] > places[shift] if scan < 2 else places[other] < places[shift]
                        term = jnp.where(beyond, factor_of(gathered[other], (part,), scan), 1.0) * term
                total = term if total is None else total + term
            out_ref[part, rows_of(scan)] = total
        products = [factor_of(gathered[0], (part,), scan) for scan in range(2)]
        for shift in range(1, chips):
            products = [products[scan] * factor_of(gathered[shift], (part,), scan) for scan in range(2)]
        put_factors(out_ref, (part,), *products)


def half_of(plane, level):
    return lax.rem(lax.shift_right_logical(plane, level), 2)


def hop_kernel(chips, level, last, *refs):
    (entered_ref, refs) = (refs[0], refs[1:]) if level > 0 else (None, refs)
    total_ref, got_ref, new_ref, onward_ref = refs
    _, _, plane = position(chips)
    bit, after = half_of(plane, level), half_of(plane, level + 1)
    for part in range(got_ref.shape[0]):
        totals, weights = [], []
        for scan in range(4):
            got, own = got_ref[part, rows_of(scan)], total_ref[part, rows_of(scan)]
            near, far = factor_of(total_ref, (part,), scan), factor_of(got_ref, (part,), scan)
            later = bit == 1 if scan < 2 else bit == 0
            if level > 0:
                entered, weight = entered_ref[part, rows_of(scan)], entered_ref[part, pl.ds(4 * STATES + scan, 1)]
            else:
                entered, weight = jnp.zeros_like(got), jnp.ones_like(far)
            new_ref[part, rows_of(scan)] = jnp.where(later, entered + weight * got, entered)
            weights.append(jnp.where(later, weight * far, weight))
            totals.append(jnp.where(later, own + near * got, got + far * own))
        new_ref[part, pl.ds(4 * STATES, 8)] = jnp.concatenate(weights + [jnp.zeros((4, LANES), F32)], axis=0)
        if last:
            for scan in range(2):
                onward_ref[part, rows_of(scan)] = jnp.where(after == 0, totals[scan], totals[scan + 2])
        else:
            for scan in range(4):
                onward_ref[part, rows_of(scan)] = totals[scan]
            both = [factor_of(total_ref, (part,), scan) * factor_of(got_ref, (part,), scan) for scan in range(2)]
            put_factors(onward_ref, (part,), *both)


def spread_kernel(chips, level, entered_ref, got_ref, *refs):
    gathered, outs = refs[:chips], refs[chips:]
    _, chip, plane = position(chips)
    bit = half_of(plane, level)
    places = [lax.rem(chip + shift, chips) for shift in range(chips)]
    for part in range(got_ref.shape[0]):
        for scan in range(4):
            weight = entered_ref[part, pl.ds(4 * STATES + scan, 1)]
            later = bit == 1 if scan < 2 else bit == 0
            value = entered_ref[part, rows_of(scan)]
            value = jnp.where(later, value + weight * got_ref[part, rows_of(scan % 2)], value)
            whole = [factor_of(gathered[shift], (part,), scan) for shift in range(chips)]

            def before(a, b):
                return places[a] < places[b] if scan < 2 else places[a] > places[b]

            for target in range(chips):
                total = value
                for other in range(chips):
                    if other != target:
                        total = jnp.where(before(other, target), whole[other], 1.0) * total
                for source in range(chips):
                    if source == target:
                        continue
                    term = gathered[source][part, rows_of(scan)]
                    for other in range(chips):
                        if other not in (source, target):
                            between = before(source, other) & before(other, target)
                            term = jnp.where(between, whole[other], 1.0) * term
                    total = jnp.where(before(source, target), total + term, total)
                outs[target][part, rows_of(scan)] = total


def core_kernel(chips, keep_ref, got_ref, *refs):
    entered, (own_ref, send_ref) = refs[:chips], refs[chips:]
    core, chip, _ = position(chips)
    for shift in range(chips):
        owner = lax.rem(chip + chips - shift, chips)
        for part in range(keep_ref.shape[1]):
            at = (owner, part)
            for scan in range(4):
                value = entered[shift][part, rows_of(scan)]
                mine, other = keep_ref[(*at, rows_of(scan))], got_ref[(*at, rows_of(scan))]
                near = core == 0 if scan < 2 else core == 1
                to_own = factor_of(got_ref, at, scan) * value + other
                to_other = factor_of(keep_ref, at, scan) * value + mine
                own_ref[(*at, rows_of(scan))] = jnp.where(near, value, to_own)
                send_ref[(*at, rows_of(scan))] = jnp.where(near, to_other, value)


class Block:
    def __init__(self, given):
        deltas, write, read = given.deltas, given.write, given.read
        length, states = deltas.shape[0], write.shape[1]
        tables = block_tables(deltas, given.log_rates, given.resets, lax.axis_index("seq") * length)
        self.rates, self.lam, self.cum, self.lower, self.upper, seg_f, seg_r = tables
        self.mask_f = (self.lower > 0.0) & (seg_f[0] == seg_f[1])
        self.mask_r = (self.upper > 0.0) & (seg_r[0] == seg_r[1])
        seg_fc, seg_rc = seg_f[0][:, :states], seg_r[0][:, :states]
        self.end_f, self.end_r = seg_fc == seg_fc[length - 1 : length], seg_rc == seg_rc[0:1]
        self.start_f, self.start_r = seg_fc == 0.0, seg_rc == 0.0
        zero = jnp.zeros_like(write)
        self.write, self.read = write, read
        self.write_f, self.write_r = jnp.where(self.end_f, write, zero), jnp.where(self.end_r, write, zero)
        self.read_f, self.read_r = jnp.where(self.start_f, read, zero), jnp.where(self.start_r, read, zero)
        self.open_f = jnp.where(seg_f[0][length - 1 : length, 0:1] == 0.0, 1.0, 0.0)
        self.open_r = jnp.where(seg_r[0][0:1, 0:1] == 0.0, 1.0, 0.0)


def reduced(flows, collect):
    high, low = halves(flows)
    return mm(high, collect, NT) + mm(low, collect, NT)


def inner_kernel(heads, states, x_ref, cot_ref, pack_ref, *outs):
    y_ref, g_ref, flow_ref, gread_ref, gwrite_ref, rate_ref = outs[-6:]
    length, channels = x_ref.shape
    given = Packed(pack_ref, heads, states)
    deltas, own = given.deltas, Block(given)
    scores = mm(own.read, own.write, NT)
    scores_f = jnp.where(own.mask_f, scores, 0.0).astype(BF16)
    scores_r = jnp.where(own.mask_r, scores, 0.0).astype(BF16)
    parts = spread_parts(factors(deltas, own.lam, own.cum) + [own.cum, own.cum - own.lam])
    flow = jnp.zeros((3 * length, heads), F32)
    pair_f = jnp.zeros((length, length), F32)
    pair_r = jnp.zeros((length, length), F32)
    for start in range(0, channels, WIDE):
        expand = expander(heads, WIDE, start)
        spread = mm(parts, expand)
        step, u_f, v_f, u_r, v_r, cum, before = (spread[i * length : (i + 1) * length] for i in range(7))
        lanes = slice(start, start + WIDE)
        x = x_ref[:, lanes].astype(F32)
        cot = cot_ref[:, lanes].astype(F32)
        scaled = (step * x).astype(BF16).astype(F32)
        whole, chain = cum[length - 1 : length], u_f[length - 1 : length]
        wide_sf, wide_sr, wide_cf, wide_cr = v_f * scaled, v_r * scaled, u_f * cot, u_r * cot
        sc_f, sc_r, ct_f, ct_r = (value.astype(BF16) for value in (wide_sf, wide_sr, wide_cf, wide_cr))
        pre_f, pre_r = mm(scores_f, sc_f), mm(scores_r, sc_r)
        y_f, y_r = u_f * pre_f, u_r * pre_r
        g_f, g_r = v_f * mm(scores_f, ct_f, TN), v_r * mm(scores_r, ct_r, TN)
        grad = g_f + g_r
        y_ref[:, lanes] = (y_f + y_r).astype(BF16)
        g_ref[:, lanes] = grad.astype(BF16)
        flow = flow + reduced(jnp.concatenate([cot * y_f - scaled * g_f, cot * y_r - scaled * g_r, x * grad], axis=0), expand[:heads])
        pair_f = pair_f + mm(ct_f, sc_f, NT)
        pair_r = pair_r + mm(ct_r, sc_r, NT)
        from_end = whole - cum
        centre, centre_r = cum - 0.5 * whole, before - 0.5 * whole
        within = centre * wide_cf * pre_f - wide_cf * mm(scores_f, (centre * wide_sf).astype(BF16))
        within = within + wide_cr * mm(scores_r, (centre_r * wide_sr).astype(BF16)) - centre_r * wide_cr * pre_r
        at = start // WIDE
        rate_ref[at, 0:states] = mm(own.read_f, (cum * wide_cf).astype(BF16), TN)
        rate_ref[at, states : 2 * states] = mm(own.write_r, (before * wide_sr).astype(BF16), TN)
        rate_ref[at, 2 * states : 3 * states] = mm(own.write_f, (from_end * wide_sf).astype(BF16), TN) * chain
        rate_ref[at, 3 * states : 4 * states] = mm(own.read_r, ((whole - before) * wide_cr).astype(BF16), TN) * chain
        tail = [own.open_f * chain * whole, own.open_r * chain * whole, jnp.sum(within, axis=0, keepdims=True)]
        tail = tail + [jnp.sum(x * cot, axis=0, keepdims=True), jnp.zeros((4, WIDE), F32)]
        rate_ref[at, 4 * states : 4 * states + 8] = jnp.concatenate(tail, axis=0)
    pairs = (jnp.where(own.mask_f, pair_f, 0.0) + jnp.where(own.mask_r, pair_r, 0.0)).astype(BF16)
    gread_ref[...] = mm(pairs, own.write)
    gwrite_ref[...] = mm(pairs, own.read, TN)
    flow_ref[...] = flow


def entering_states(own, got, start, chips):
    core = lax.rem(lax.axis_index("seq"), 2)
    chunk, part, chip = place_of(start, own[0].shape[1], chips)
    values = []
    for scan in range(4):
        a, b = own[chunk][chip, part, rows_of(scan)], got[chunk][chip, part, rows_of(scan)]
        values.append(jnp.concatenate([jnp.where(core == 0, a, b), jnp.where(core == 0, b, a)], axis=1))
    return values


def rates_kernel(chunks, chips, rate_ref, *refs):
    own, got, small_ref = refs[:chunks], refs[chunks : 2 * chunks], refs[2 * chunks]
    heads = small_ref.shape[1]
    total = jnp.zeros((8, heads), F32)
    for at in range(rate_ref.shape[0]):
        in_f, back_r, back_f, in_r = entering_states(own, got, at * WIDE, chips)
        tail = rate_ref[at, pl.ds(4 * STATES, 8)]
        met = sum(value * rate_ref[at, rows_of(scan)] for scan, value in enumerate((in_f, back_r, back_f, in_r)))
        met = met + tail[0:1] * (in_f * back_f) + tail[1:2] * (in_r * back_r)
        met = jnp.sum(met, axis=0, keepdims=True) + tail[2:3]
        rows = jnp.concatenate([met, tail[3:4], jnp.zeros((6, WIDE), F32)], axis=0)
        collect = expander(heads, WIDE, at * WIDE)[:heads]
        for piece in thirds(rows):
            total = total + mm(piece, collect, NT)
    small_ref[...] = total[:2]


def finish_kernel(chunks, chips, heads, states, x_ref, cot_ref, pack_ref, *refs):
    y_ref, g_ref, flow_ref, gread0_ref, gwrite0_ref = refs[:5]
    entered, got = refs[5 : 5 + chunks], refs[5 + chunks : 5 + 2 * chunks]
    out_ref, gin_ref, steps_ref, gwrite_ref, gread_ref = refs[5 + 2 * chunks :]
    length, channels = x_ref.shape
    given = Packed(pack_ref, heads, states)
    deltas, own = given.deltas, Block(given)
    skip = jnp.broadcast_to(given.skip, (8, heads))
    parts = spread_parts(factors(deltas, own.lam, own.cum) + [skip])
    flow = flow_ref[...]
    rows = jnp.zeros((8, heads), F32)
    acc_read_f = jnp.zeros((length, states), F32)
    acc_read_r = jnp.zeros((length, states), F32)
    acc_write_f = jnp.zeros((length, states), F32)
    acc_write_r = jnp.zeros((length, states), F32)
    for start in range(0, channels, WIDE):
        expand = expander(heads, WIDE, start)
        spread = mm(parts, expand)
        step, u_f, v_f, u_r, v_r = (spread[i * length : (i + 1) * length] for i in range(5))
        gain = spread[5 * length : 5 * length + 1]
        lanes = slice(start, start + WIDE)
        x = x_ref[:, lanes].astype(F32)
        cot = cot_ref[:, lanes].astype(F32)
        scaled = (step * x).astype(BF16).astype(F32)
        chain = u_f[length - 1 : length]
        sc_f, sc_r = (v_f * scaled).astype(BF16), (v_r * scaled).astype(BF16)
        ct_f, ct_r = (u_f * cot).astype(BF16), (u_r * cot).astype(BF16)
        in_f, back_r, back_f, in_r = entering_states(entered, got, start, chips)
        in_f16, in_r16 = in_f.astype(BF16), (in_r * chain).astype(BF16)
        back_f16, back_r16 = (back_f * chain).astype(BF16), back_r.astype(BF16)
        y_f, y_r = u_f * mm(own.read_f, in_f16), u_r * mm(own.read_r, in_r16)
        g_f, g_r = v_f * mm(own.write_f, back_f16), v_r * mm(own.write_r, back_r16)
        out_ref[:, lanes] = (y_ref[:, lanes] + (y_f + y_r) + gain * x).astype(BF16)
        grad = g_f + g_r
        gin_ref[:, lanes] = (step * (g_ref[:, lanes] + grad) + gain * cot).astype(BF16)
        local_f, local_r = mm(own.write_f, sc_f, TN) * chain, mm(own.write_r, sc_r, TN)
        through = back_f * (local_f + own.open_f * chain * in_f) + back_r * (local_r + own.open_r * chain * in_r)
        through = jnp.sum(through, axis=0, keepdims=True)
        small = jnp.concatenate([through, jnp.zeros((7, WIDE), F32)], axis=0)
        sums = reduced(jnp.concatenate([cot * y_f - scaled * g_f, cot * y_r - scaled * g_r, x * grad, small], axis=0), expand[:heads])
        flow = flow + sums[: 3 * length]
        rows = rows + sums[3 * length :]
        acc_read_f = acc_read_f + mm(ct_f, in_f16, NT)
        acc_read_r = acc_read_r + mm(ct_r, in_r16, NT)
        acc_write_f = acc_write_f + mm(sc_f, back_f16, NT)
        acc_write_r = acc_write_r + mm(sc_r, back_r16, NT)
    gread = gread0_ref[...] + jnp.where(own.start_f, acc_read_f, 0.0) + jnp.where(own.start_r, acc_read_r, 0.0)
    gwrite = gwrite0_ref[...] + jnp.where(own.end_f, acc_write_f, 0.0) + jnp.where(own.end_r, acc_write_r, 0.0)
    gread_ref[...] = gread.T
    gwrite_ref[...] = gwrite.T
    logs = exact(own.upper, flow[:length]) + exact(own.lower, flow[length : 2 * length]) + rows[0:1]
    steps_ref[...] = (flow[2 * length :] - own.rates * logs).T


def call(body, out_shape, spaces, flops, size, name, scratch=(), room=16):
    return pl.pallas_call(
        body,
        out_shape=out_shape,
        in_specs=[pl.BlockSpec(memory_space=space) for space in spaces],
        out_specs=jax.tree.map(lambda _: pl.BlockSpec(memory_space=pltpu.VMEM), out_shape),
        scratch_shapes=scratch,
        compiler_params=pltpu.CompilerParams(vmem_limit_bytes=room << 20),
        cost_estimate=pl.CostEstimate(flops=flops, bytes_accessed=size, transcendentals=0),
        name=name,
    )


def local(chips, inputs, step_sizes, write_vecs, read_vecs, log_rates, skip_gain, resets, cotangent):
    x, cot = inputs[0], cotangent[0]
    deltas, write, read = step_sizes[0].T, write_vecs[0].T, read_vecs[0].T
    length, channels = x.shape
    heads, states = deltas.shape[0], write.shape[0]
    devices = lax.axis_size("seq")
    planes = devices // (2 * chips)
    levels = int(math.log2(planes))
    chunks = min(CHUNKS, channels // (WIDE * chips))
    parts = channels // (WIDE * chips * chunks)
    lined = [jnp.pad(row.astype(F32)[None], ((0, 0), (0, length - row.shape[0]))) for row in (log_rates, skip_gain, resets[0])]
    pack = jnp.concatenate([deltas, write.astype(F32), read.astype(F32), *lined, jnp.zeros((5, length), F32)], axis=0)

    def like(*shape, kind=F32):
        return jax.ShapeDtypeStruct(shape, kind)

    vmem = pltpu.VMEM
    message, plain = 4 * states + 8, 4 * states
    group = like(chips, parts, message, LANES)
    single = like(parts, message, LANES)
    half = like(parts, 2 * states, LANES)
    bare = like(parts, plain, LANES)
    pair = like(chips, parts, plain, LANES)
    made = call(
        functools.partial(states_kernel, chunks, chips, heads, states),
        [group] * (2 * chunks),
        [pl.ANY] * 2 + [vmem],
        300 * 10**6,
        4 * 10**6,
        "states",
        [
            pltpu.VMEM((length, channels), BF16),
            pltpu.VMEM((length, channels), BF16),
            pltpu.SemaphoreType.DMA((2, channels // WIDE)),
        ],
        ROOM,
    )(x, cot, pack)
    keep, send = made[:chunks], made[chunks:]

    def device(plane, chip, core):
        return (plane * chips + chip) * 2 + core

    every = [(p, a, c) for p in range(planes) for a in range(chips) for c in range(2)]
    swap = [(device(p, a, c), device(p, a, 1 - c)) for p, a, c in every]

    def turn(shift):
        return [(device(p, a, c), device(p, (a + shift) % chips, c)) for p, a, c in every]

    def across(level):
        return [(device(p, a, c), device(p ^ 2**level, a, c)) for p, a, c in every]

    def send_to(value, perm):
        return lax.ppermute(value, "seq", perm)

    gots, chipped = [], []
    for k in range(chunks):
        gots.append(send_to(send[k], swap))
        chipped.append(call(functools.partial(chip_kernel, chips), [single] * chips, [vmem] * 2, 10**6, 10**6, "chip")(keep[k], gots[k]))
    inner = call(
        functools.partial(inner_kernel, heads, states),
        [
            like(length, channels, kind=BF16),
            like(length, channels, kind=BF16),
            like(3 * length, heads),
            like(length, states),
            like(length, states),
            like(channels // WIDE, message, WIDE),
        ],
        [vmem] * 3 + [pl.ANY] * chunks,
        10**9,
        8 * 10**6,
        "inner",
    )(x, cot, pack, *[value[0] for value in chipped])
    size = 4 * parts * states * LANES * 4
    owns, theirs_in = [], []
    for k in range(chunks):
        got, chip_totals = gots[k], chipped[k]
        gathered = [chip_totals[0]] + [None] * (chips - 1)
        for shift in range(1, chips):
            gathered[chips - shift] = send_to(chip_totals[shift], turn(shift))
        onward = call(functools.partial(plane_kernel, chips), single, [pl.ANY] + [vmem] * chips, 10**6, size * 3, "plane")(inner[3], *gathered)
        before = []
        for level in range(levels - 1):
            arrived = send_to(onward, across(level))
            last = level == levels - 2
            hop = call(
                functools.partial(hop_kernel, chips, level, last),
                [single, half if last else single],
                [vmem] * (2 + len(before)),
                10**6,
                size * 4,
                "hop",
            )
            entry, onward = hop(*before, onward, arrived)
            before = [entry]
        arrived = send_to(onward, across(levels - 1))
        placed = call(
            functools.partial(spread_kernel, chips, levels - 1), [bare] * chips, [vmem] * (2 + chips), 10**6, size * 5, "spread"
        )(*before, arrived, *gathered)
        entered = [placed[0]] + [send_to(placed[shift], turn(shift)) for shift in range(1, chips)]
        mine, theirs = call(functools.partial(core_kernel, chips), [pair] * 2, [vmem] * (2 + chips), 10**6, size * 8, "core")(
            keep[k], got, *entered
        )
        owns.append(mine)
        theirs_in.append(send_to(theirs, swap))

    small = call(
        functools.partial(rates_kernel, chunks, chips), like(2, heads), [vmem] * (1 + 2 * chunks), 10**6, 4 * 10**6, "rates"
    )(inner[5], *owns, *theirs_in)
    count = devices * lax.axis_size("dp")
    copies = jnp.broadcast_to(small[None], (count,) + small.shape)
    total = jnp.sum(lax.all_to_all(copies, ("seq", "dp"), 0, 0, tiled=True), axis=0)
    outputs, grad_inputs, grad_steps, grad_write, grad_read = call(
        functools.partial(finish_kernel, chunks, chips, heads, states),
        [
            like(length, channels, kind=BF16),
            like(length, channels, kind=BF16),
            like(heads, length),
            like(states, length),
            like(states, length),
        ],
        [vmem] * (8 + 2 * chunks),
        2 * 10**9,
        6 * 10**6,
        "finish",
    )(x, cot, pack, *inner[:5], *owns, *theirs_in)
    return (outputs[None], grad_inputs[None], grad_steps.T[None], grad_write.T[None], grad_read.T[None], total[0], total[1])


def solution(mesh):
    along = P("dp", "seq", None)
    chips = 2 ** (int(math.log2(mesh.shape["seq"] // 2)) // 2)
    return jax.shard_map(
        functools.partial(local, chips),
        mesh=mesh,
        in_specs=(along, along, along, along, P(), P(), P("dp", None), along),
        out_specs=(along, along, along, along, along, P(), P()),
        check_vma=False,
    )
```

```python
import functools
import math

import jax
import jax.numpy as jnp
from jax import lax
from jax.experimental import pallas as pl
from jax.experimental.pallas import tpu as pltpu
from jax.sharding import PartitionSpec as P

F32 = jnp.float32
BF16 = jnp.bfloat16
LANES = 128
WIDE = 256
STATES = 64
RESETS = 8
MEMBERS = 1
CHUNKS = 4
ROOM = 52
NN = (((1,), (0,)), ((), ()))
NT = (((1,), (1,)), ((), ()))
TN = (((0,), (0,)), ((), ()))


def mm(a, b, dims=NN):
    return lax.dot_general(a, b, dims, preferred_element_type=F32)


def exact(a, b):
    return jnp.dot(a, b, precision=lax.Precision.HIGHEST, preferred_element_type=F32)


def halves(value):
    upper = value.astype(BF16)
    return upper, (value - upper.astype(F32)).astype(BF16)


def thirds(value):
    upper = value.astype(BF16)
    rest = value - upper.astype(F32)
    middle = rest.astype(BF16)
    return upper, middle, (rest - middle.astype(F32)).astype(BF16)


def iota(shape, dim):
    return lax.broadcasted_iota(jnp.int32, shape, dim)


def block_tables(deltas, log_rates, resets, first):
    length = deltas.shape[0]
    square = (length, length)
    row, col = iota(square, 0), iota(square, 1)
    lower = (row >= col).astype(F32)
    upper = (row <= col).astype(F32)
    rates = jnp.exp(log_rates)
    lam = -deltas * rates
    cum = exact(lower, lam)

    def marks(grid, ahead):
        hit = jnp.zeros(square, jnp.bool_)
        for k in range(RESETS):
            hit = hit | (grid + (first + ahead) == resets[0:1, k : k + 1])
        return hit.astype(BF16)

    low16, up16 = lower.astype(BF16), upper.astype(BF16)
    seg_f = mm(low16, marks(row, 0)), mm(marks(col, 0), up16)
    seg_r = mm(up16, marks(row, 1)), mm(marks(col, 1), low16)
    return rates, lam, cum, lower, upper, seg_f, seg_r


def expander(heads, width, start):
    shape = (3 * heads, width)
    per_head = 2 * LANES // 4
    return (iota(shape, 0) % heads == (iota(shape, 1) + start) // per_head).astype(BF16)


def spread_parts(values):
    return jnp.concatenate([jnp.concatenate(thirds(v), axis=1) for v in values], axis=0)


def factors(deltas, lam, cum):
    before = cum - lam
    return [deltas, jnp.exp(cum), jnp.exp(-cum), jnp.exp(-before), jnp.exp(before)]


def place_of(start, parts, chips):
    part, chip = divmod(start // WIDE, chips)
    return part // parts, part % parts, chip


class Packed:
    def __init__(self, pack_ref, heads, states):
        self.deltas = pack_ref[0:heads].T
        self.write = pack_ref[heads : heads + states].T.astype(BF16)
        self.read = pack_ref[heads + states : heads + 2 * states].T.astype(BF16)
        rows = heads + 2 * states
        row = pack_ref[rows : rows + 1]
        self.log_rates = row[:, 0:heads]
        self.skip = row[:, heads : 2 * heads]
        self.resets = row[:, 2 * heads : 2 * heads + RESETS].astype(jnp.int32)


def states_kernel(chunks, chips, heads, states, x_hbm, cot_hbm, pack_ref, *refs):
    outs, (x_ref, cot_ref, wide_sem) = refs[: 2 * chunks], refs[2 * chunks :]
    length, channels = x_ref.shape
    starts = range(0, channels, WIDE)
    wides = [
        [
            pltpu.make_async_copy(source.at[:, pl.ds(start, WIDE)], target.at[:, pl.ds(start, WIDE)], wide_sem.at[i, start // WIDE])
            for i, (source, target) in enumerate(((x_hbm, x_ref), (cot_hbm, cot_ref)))
        ]
        for start in starts
    ]
    for both in wides:
        for copy in both:
            copy.start()
    index = lax.axis_index("seq")
    core = lax.rem(index, 2)
    given = Packed(pack_ref, heads, states)
    deltas = given.deltas
    rates, lam, cum, lower, upper, seg_f, seg_r = block_tables(deltas, given.log_rates, given.resets, index * length)
    seg_fc, seg_rc = seg_f[0][:, :states], seg_r[0][:, :states]
    write, read = given.write, given.read
    zero = jnp.zeros_like(write)
    write_f = jnp.where(seg_fc == seg_fc[length - 1 : length], write, zero)
    write_r = jnp.where(seg_rc == seg_rc[0:1], write, zero)
    read_f = jnp.where(seg_fc == 0.0, read, zero)
    read_r = jnp.where(seg_rc == 0.0, read, zero)
    open_f = jnp.where(seg_f[0][length - 1 : length, 0:1] == 0.0, 1.0, 0.0)
    open_r = jnp.where(seg_r[0][0:1, 0:1] == 0.0, 1.0, 0.0)
    parts = spread_parts(factors(deltas, lam, cum))
    keep, send = outs[:chunks], outs[chunks:]
    for start in starts:
        spread = mm(parts, expander(heads, WIDE, start))
        for copy in wides[start // WIDE]:
            copy.wait()
        step, u_f, v_f, u_r, v_r = (spread[i * length : (i + 1) * length] for i in range(5))
        lanes = slice(start, start + WIDE)
        scaled = (step * x_ref[:, lanes].astype(F32)).astype(BF16).astype(F32)
        cot = cot_ref[:, lanes].astype(F32)
        chain = u_f[length - 1 : length]
        carry_f = mm(write_f, (v_f * scaled).astype(BF16), TN) * chain
        carry_r = mm(write_r, (v_r * scaled).astype(BF16), TN)
        adj_f = mm(read_f, (u_f * cot).astype(BF16), TN)
        adj_r = mm(read_r, (u_r * cot).astype(BF16), TN) * chain
        tail = jnp.concatenate([open_f * chain, open_r * chain, jnp.zeros((6, WIDE), F32)], axis=0)
        chunk, part, chip = place_of(start, keep[0].shape[1], chips)
        rows = 0
        for value in (carry_f, adj_r, adj_f, carry_r, tail):
            zeroth, other = value[:, :LANES], value[:, LANES:]
            span = pl.ds(rows, value.shape[0])
            keep[chunk][chip, part, span] = jnp.where(core == 0, zeroth, other)
            send[chunk][chip, part, span] = jnp.where(core == 0, other, zeroth)
            rows += value.shape[0]


def position(chips):
    index = lax.axis_index("seq")
    core = lax.rem(index, 2)
    chip = lax.rem(lax.div(index, 2), chips)
    return core, chip, lax.div(index, 2 * chips)


def rows_of(scan):
    return pl.ds(scan * STATES, STATES)


def factor_of(ref, at, scan):
    return ref[(*at, pl.ds(4 * STATES + scan % 2, 1))]


def put_factors(ref, at, forward, reverse):
    ref[(*at, pl.ds(4 * STATES, 8))] = jnp.concatenate([forward, reverse, jnp.zeros((6, LANES), F32)], axis=0)


def chip_kernel(chips, keep_ref, got_ref, *outs):
    core, chip, _ = position(chips)
    for shift in range(chips):
        owner = lax.rem(chip + shift, chips)
        for part in range(keep_ref.shape[1]):
            at = (owner, part)
            for scan in range(4):
                mine, other = keep_ref[(*at, rows_of(scan))], got_ref[(*at, rows_of(scan))]
                own, far = factor_of(keep_ref, at, scan), factor_of(got_ref, at, scan)
                later = core == 1 if scan < 2 else core == 0
                outs[shift][part, rows_of(scan)] = jnp.where(later, mine + own * other, other + far * mine)
            both = [factor_of(keep_ref, at, scan) * factor_of(got_ref, at, scan) for scan in range(2)]
            put_factors(outs[shift], (part,), *both)


def plane_kernel(chips, members, *refs):
    out_ref = refs[members * chips]
    parts = out_ref.shape[0] // members
    for member in range(members):
        plane_totals(chips, refs[member * chips : (member + 1) * chips], out_ref.at[pl.ds(member * parts, parts)])


def plane_totals(chips, gathered, out_ref):
    _, chip, _ = position(chips)
    places = [lax.rem(chip + shift, chips) for shift in range(chips)]
    for part in range(out_ref.shape[0]):
        for scan in range(4):
            total = None
            for shift in range(chips):
                term = gathered[shift][part, rows_of(scan)]
                for other in range(chips):
                    if other != shift:
                        beyond = places[other] > places[shift] if scan < 2 else places[other] < places[shift]
                        term = jnp.where(beyond, factor_of(gathered[other], (part,), scan), 1.0) * term
                total = term if total is None else total + term
            out_ref[part, rows_of(scan)] = total
        products = [factor_of(gathered[0], (part,), scan) for scan in range(2)]
        for shift in range(1, chips):
            products = [products[scan] * factor_of(gathered[shift], (part,), scan) for scan in range(2)]
        put_factors(out_ref, (part,), *products)


def half_of(plane, level):
    return lax.rem(lax.shift_right_logical(plane, level), 2)


def hop_kernel(chips, members, level, last, *refs):
    *given, new_ref, onward_ref = refs
    given = given[: len(given) // members * members] if members > 1 else given[: 2 + (level > 0)]
    each = len(given) // members
    parts = new_ref.shape[0] // members
    for member in range(members):
        span = pl.ds(member * parts, parts)
        mine = given[member * each : (member + 1) * each]
        hop_member(chips, level, last, *([None] * (3 - each)), *mine, new_ref.at[span], onward_ref.at[span])


def hop_member(chips, level, last, entered_ref, total_ref, got_ref, new_ref, onward_ref):
    _, _, plane = position(chips)
    bit, after = half_of(plane, level), half_of(plane, level + 1)
    for part in range(got_ref.shape[0]):
        totals, weights = [], []
        for scan in range(4):
            got, own = got_ref[part, rows_of(scan)], total_ref[part, rows_of(scan)]
            near, far = factor_of(total_ref, (part,), scan), factor_of(got_ref, (part,), scan)
            later = bit == 1 if scan < 2 else bit == 0
            if level > 0:
                entered, weight = entered_ref[part, rows_of(scan)], entered_ref[part, pl.ds(4 * STATES + scan, 1)]
            else:
                entered, weight = jnp.zeros_like(got), jnp.ones_like(far)
            new_ref[part, rows_of(scan)] = jnp.where(later, entered + weight * got, entered)
            weights.append(jnp.where(later, weight * far, weight))
            totals.append(jnp.where(later, own + near * got, got + far * own))
        new_ref[part, pl.ds(4 * STATES, 8)] = jnp.concatenate(weights + [jnp.zeros((4, LANES), F32)], axis=0)
        if last:
            for scan in range(2):
                onward_ref[part, rows_of(scan)] = jnp.where(after == 0, totals[scan], totals[scan + 2])
        else:
            for scan in range(4):
                onward_ref[part, rows_of(scan)] = totals[scan]
            both = [factor_of(total_ref, (part,), scan) * factor_of(got_ref, (part,), scan) for scan in range(2)]
            put_factors(onward_ref, (part,), *both)


def spread_kernel(chips, members, level, *refs):
    entered_ref, got_ref, *refs = refs
    parts = got_ref.shape[0] // members
    for member in range(members):
        span = pl.ds(member * parts, parts)
        gathered = refs[member * chips : (member + 1) * chips]
        outs = refs[(members + member) * chips : (members + member + 1) * chips]
        spread_member(chips, level, entered_ref.at[span], got_ref.at[span], gathered, outs)


def spread_member(chips, level, entered_ref, got_ref, gathered, outs):
    _, chip, plane = position(chips)
    bit = half_of(plane, level)
    places = [lax.rem(chip + shift, chips) for shift in range(chips)]
    for part in range(got_ref.shape[0]):
        for scan in range(4):
            weight = entered_ref[part, pl.ds(4 * STATES + scan, 1)]
            later = bit == 1 if scan < 2 else bit == 0
            value = entered_ref[part, rows_of(scan)]
            value = jnp.where(later, value + weight * got_ref[part, rows_of(scan % 2)], value)
            whole = [factor_of(gathered[shift], (part,), scan) for shift in range(chips)]

            def before(a, b):
                return places[a] < places[b] if scan < 2 else places[a] > places[b]

            for target in range(chips):
                total = value
                for other in range(chips):
                    if other != target:
                        total = jnp.where(before(other, target), whole[other], 1.0) * total
                for source in range(chips):
                    if source == target:
                        continue
                    term = gathered[source][part, rows_of(scan)]
                    for other in range(chips):
                        if other not in (source, target):
                            between = before(source, other) & before(other, target)
                            term = jnp.where(between, whole[other], 1.0) * term
                    total = jnp.where(before(source, target), total + term, total)
                outs[target][part, rows_of(scan)] = total


def core_kernel(chips, extra, *refs):
    keep_ref, got_ref, *refs = refs[extra:]
    entered, (own_ref, send_ref) = refs[:chips], refs[chips:]
    core, chip, _ = position(chips)
    for shift in range(chips):
        owner = lax.rem(chip + chips - shift, chips)
        for part in range(keep_ref.shape[1]):
            at = (owner, part)
            for scan in range(4):
                value = entered[shift][part, rows_of(scan)]
                mine, other = keep_ref[(*at, rows_of(scan))], got_ref[(*at, rows_of(scan))]
                near = core == 0 if scan < 2 else core == 1
                to_own = factor_of(got_ref, at, scan) * value + other
                to_other = factor_of(keep_ref, at, scan) * value + mine
                own_ref[(*at, rows_of(scan))] = jnp.where(near, value, to_own)
                send_ref[(*at, rows_of(scan))] = jnp.where(near, to_other, value)


class Block:
    def __init__(self, given):
        deltas, write, read = given.deltas, given.write, given.read
        length, states = deltas.shape[0], write.shape[1]
        tables = block_tables(deltas, given.log_rates, given.resets, lax.axis_index("seq") * length)
        self.rates, self.lam, self.cum, self.lower, self.upper, seg_f, seg_r = tables
        self.mask_f = (self.lower > 0.0) & (seg_f[0] == seg_f[1])
        self.mask_r = (self.upper > 0.0) & (seg_r[0] == seg_r[1])
        seg_fc, seg_rc = seg_f[0][:, :states], seg_r[0][:, :states]
        self.end_f, self.end_r = seg_fc == seg_fc[length - 1 : length], seg_rc == seg_rc[0:1]
        self.start_f, self.start_r = seg_fc == 0.0, seg_rc == 0.0
        zero = jnp.zeros_like(write)
        self.write, self.read = write, read
        self.write_f, self.write_r = jnp.where(self.end_f, write, zero), jnp.where(self.end_r, write, zero)
        self.read_f, self.read_r = jnp.where(self.start_f, read, zero), jnp.where(self.start_r, read, zero)
        self.open_f = jnp.where(seg_f[0][length - 1 : length, 0:1] == 0.0, 1.0, 0.0)
        self.open_r = jnp.where(seg_r[0][0:1, 0:1] == 0.0, 1.0, 0.0)


def reduced(flows, collect):
    high, low = halves(flows)
    return mm(high, collect, NT) + mm(low, collect, NT)


def inner_kernel(heads, states, x_ref, cot_ref, pack_ref, *outs):
    flow_ref, gread_ref, gwrite_ref, rate_ref = outs[-4:]
    length, channels = x_ref.shape
    given = Packed(pack_ref, heads, states)
    deltas, own = given.deltas, Block(given)
    scores = mm(own.read, own.write, NT)
    scores_f = jnp.where(own.mask_f, scores, 0.0).astype(BF16)
    scores_r = jnp.where(own.mask_r, scores, 0.0).astype(BF16)
    parts = spread_parts(factors(deltas, own.lam, own.cum) + [own.cum, own.cum - own.lam])
    flow = jnp.zeros((3 * length, heads), F32)
    pair_f = jnp.zeros((length, length), F32)
    pair_r = jnp.zeros((length, length), F32)
    for start in range(0, channels, WIDE):
        expand = expander(heads, WIDE, start)
        spread = mm(parts, expand)
        step, u_f, v_f, u_r, v_r, cum, before = (spread[i * length : (i + 1) * length] for i in range(7))
        lanes = slice(start, start + WIDE)
        x = x_ref[:, lanes].astype(F32)
        cot = cot_ref[:, lanes].astype(F32)
        scaled = (step * x).astype(BF16).astype(F32)
        whole, chain = cum[length - 1 : length], u_f[length - 1 : length]
        wide_sf, wide_sr, wide_cf, wide_cr = v_f * scaled, v_r * scaled, u_f * cot, u_r * cot
        sc_f, sc_r, ct_f, ct_r = (value.astype(BF16) for value in (wide_sf, wide_sr, wide_cf, wide_cr))
        pre_f, pre_r = mm(scores_f, sc_f), mm(scores_r, sc_r)
        y_f, y_r = u_f * pre_f, u_r * pre_r
        g_f, g_r = v_f * mm(scores_f, ct_f, TN), v_r * mm(scores_r, ct_r, TN)
        grad = g_f + g_r
        flow = flow + reduced(jnp.concatenate([cot * y_f - scaled * g_f, cot * y_r - scaled * g_r, x * grad], axis=0), expand[:heads])
        pair_f = pair_f + mm(ct_f, sc_f, NT)
        pair_r = pair_r + mm(ct_r, sc_r, NT)
        from_end = whole - cum
        centre, centre_r = cum - 0.5 * whole, before - 0.5 * whole
        within = centre * wide_cf * pre_f - wide_cf * mm(scores_f, (centre * wide_sf).astype(BF16))
        within = within + wide_cr * mm(scores_r, (centre_r * wide_sr).astype(BF16)) - centre_r * wide_cr * pre_r
        at = start // WIDE
        rate_ref[at, 0:states] = mm(own.read_f, (cum * wide_cf).astype(BF16), TN)
        rate_ref[at, states : 2 * states] = mm(own.write_r, (before * wide_sr).astype(BF16), TN)
        rate_ref[at, 2 * states : 3 * states] = mm(own.write_f, (from_end * wide_sf).astype(BF16), TN) * chain
        rate_ref[at, 3 * states : 4 * states] = mm(own.read_r, ((whole - before) * wide_cr).astype(BF16), TN) * chain
        tail = [own.open_f * chain * whole, own.open_r * chain * whole, jnp.sum(within, axis=0, keepdims=True)]
        tail = tail + [jnp.sum(x * cot, axis=0, keepdims=True), jnp.zeros((4, WIDE), F32)]
        rate_ref[at, 4 * states : 4 * states + 8] = jnp.concatenate(tail, axis=0)
    pairs = (jnp.where(own.mask_f, pair_f, 0.0) + jnp.where(own.mask_r, pair_r, 0.0)).astype(BF16)
    gread_ref[...] = mm(pairs, own.write)
    gwrite_ref[...] = mm(pairs, own.read, TN)
    flow_ref[...] = flow


def entering_states(own, got, start, chips):
    core = lax.rem(lax.axis_index("seq"), 2)
    chunk, part, chip = place_of(start, own[0].shape[1], chips)
    values = []
    for scan in range(4):
        a, b = own[chunk][chip, part, rows_of(scan)], got[chunk][chip, part, rows_of(scan)]
        values.append(jnp.concatenate([jnp.where(core == 0, a, b), jnp.where(core == 0, b, a)], axis=1))
    return values


def rates_kernel(chunks, chips, rate_ref, *refs):
    own, got, small_ref = refs[:chunks], refs[chunks : 2 * chunks], refs[2 * chunks]
    heads = small_ref.shape[1]
    total = jnp.zeros((8, heads), F32)
    for at in range(rate_ref.shape[0]):
        in_f, back_r, back_f, in_r = entering_states(own, got, at * WIDE, chips)
        tail = rate_ref[at, pl.ds(4 * STATES, 8)]
        met = sum(value * rate_ref[at, rows_of(scan)] for scan, value in enumerate((in_f, back_r, back_f, in_r)))
        met = met + tail[0:1] * (in_f * back_f) + tail[1:2] * (in_r * back_r)
        met = jnp.sum(met, axis=0, keepdims=True) + tail[2:3]
        rows = jnp.concatenate([met, tail[3:4], jnp.zeros((6, WIDE), F32)], axis=0)
        collect = expander(heads, WIDE, at * WIDE)[:heads]
        for piece in thirds(rows):
            total = total + mm(piece, collect, NT)
    small_ref[...] = total[:2]


def finish_kernel(chunks, chips, heads, states, x_ref, cot_ref, pack_ref, *refs):
    flow_ref, gread0_ref, gwrite0_ref = refs[:3]
    entered, got = refs[3 : 3 + chunks], refs[3 + chunks : 3 + 2 * chunks]
    out_ref, gin_ref, steps_ref, gwrite_ref, gread_ref = refs[3 + 2 * chunks :]
    length, channels = x_ref.shape
    given = Packed(pack_ref, heads, states)
    deltas, own = given.deltas, Block(given)
    scores = mm(own.read, own.write, NT)
    scores_f = jnp.where(own.mask_f, scores, 0.0).astype(BF16)
    scores_r = jnp.where(own.mask_r, scores, 0.0).astype(BF16)
    skip = jnp.broadcast_to(given.skip, (8, heads))
    parts = spread_parts(factors(deltas, own.lam, own.cum) + [skip])
    flow = flow_ref[...]
    rows = jnp.zeros((8, heads), F32)
    acc_read_f = jnp.zeros((length, states), F32)
    acc_read_r = jnp.zeros((length, states), F32)
    acc_write_f = jnp.zeros((length, states), F32)
    acc_write_r = jnp.zeros((length, states), F32)
    for start in range(0, channels, WIDE):
        expand = expander(heads, WIDE, start)
        spread = mm(parts, expand)
        step, u_f, v_f, u_r, v_r = (spread[i * length : (i + 1) * length] for i in range(5))
        gain = spread[5 * length : 5 * length + 1]
        lanes = slice(start, start + WIDE)
        x = x_ref[:, lanes].astype(F32)
        cot = cot_ref[:, lanes].astype(F32)
        scaled = (step * x).astype(BF16).astype(F32)
        chain = u_f[length - 1 : length]
        sc_f, sc_r = (v_f * scaled).astype(BF16), (v_r * scaled).astype(BF16)
        ct_f, ct_r = (u_f * cot).astype(BF16), (u_r * cot).astype(BF16)
        in_f, back_r, back_f, in_r = entering_states(entered, got, start, chips)
        in_f16, in_r16 = in_f.astype(BF16), (in_r * chain).astype(BF16)
        back_f16, back_r16 = (back_f * chain).astype(BF16), back_r.astype(BF16)
        y_f, y_r = u_f * mm(own.read_f, in_f16), u_r * mm(own.read_r, in_r16)
        g_f, g_r = v_f * mm(own.write_f, back_f16), v_r * mm(own.write_r, back_r16)
        inside = u_f * mm(scores_f, sc_f) + u_r * mm(scores_r, sc_r)
        inside_grad = v_f * mm(scores_f, ct_f, TN) + v_r * mm(scores_r, ct_r, TN)
        out_ref[:, lanes] = (inside + (y_f + y_r) + gain * x).astype(BF16)
        grad = g_f + g_r
        gin_ref[:, lanes] = (step * (inside_grad + grad) + gain * cot).astype(BF16)
        local_f, local_r = mm(own.write_f, sc_f, TN) * chain, mm(own.write_r, sc_r, TN)
        through = back_f * (local_f + own.open_f * chain * in_f) + back_r * (local_r + own.open_r * chain * in_r)
        through = jnp.sum(through, axis=0, keepdims=True)
        small = jnp.concatenate([through, jnp.zeros((7, WIDE), F32)], axis=0)
        sums = reduced(jnp.concatenate([cot * y_f - scaled * g_f, cot * y_r - scaled * g_r, x * grad, small], axis=0), expand[:heads])
        flow = flow + sums[: 3 * length]
        rows = rows + sums[3 * length :]
        acc_read_f = acc_read_f + mm(ct_f, in_f16, NT)
        acc_read_r = acc_read_r + mm(ct_r, in_r16, NT)
        acc_write_f = acc_write_f + mm(sc_f, back_f16, NT)
        acc_write_r = acc_write_r + mm(sc_r, back_r16, NT)
    gread = gread0_ref[...] + jnp.where(own.start_f, acc_read_f, 0.0) + jnp.where(own.start_r, acc_read_r, 0.0)
    gwrite = gwrite0_ref[...] + jnp.where(own.end_f, acc_write_f, 0.0) + jnp.where(own.end_r, acc_write_r, 0.0)
    gread_ref[...] = gread.T
    gwrite_ref[...] = gwrite.T
    logs = exact(own.upper, flow[:length]) + exact(own.lower, flow[length : 2 * length]) + rows[0:1]
    steps_ref[...] = (flow[2 * length :] - own.rates * logs).T


def call(body, out_shape, spaces, flops, size, name, scratch=(), room=16):
    return pl.pallas_call(
        body,
        out_shape=out_shape,
        in_specs=[pl.BlockSpec(memory_space=space) for space in spaces],
        out_specs=jax.tree.map(lambda _: pl.BlockSpec(memory_space=pltpu.VMEM), out_shape),
        scratch_shapes=scratch,
        compiler_params=pltpu.CompilerParams(vmem_limit_bytes=room << 20),
        cost_estimate=pl.CostEstimate(flops=flops, bytes_accessed=size, transcendentals=0),
        name=name,
    )


def local(chips, inputs, step_sizes, write_vecs, read_vecs, log_rates, skip_gain, resets, cotangent):
    x, cot = inputs[0], cotangent[0]
    deltas, write, read = step_sizes[0].T, write_vecs[0].T, read_vecs[0].T
    length, channels = x.shape
    heads, states = deltas.shape[0], write.shape[0]
    devices = lax.axis_size("seq")
    planes = devices // (2 * chips)
    levels = int(math.log2(planes))
    chunks = min(CHUNKS, channels // (WIDE * chips))
    parts = channels // (WIDE * chips * chunks)
    line = jnp.concatenate([log_rates, skip_gain, resets[0].astype(F32), jnp.zeros((length - 2 * heads - RESETS,), F32)])
    pack = jnp.concatenate([deltas, write.astype(F32), read.astype(F32), jnp.broadcast_to(line[None], (8, length))], axis=0)

    def like(*shape, kind=F32):
        return jax.ShapeDtypeStruct(shape, kind)

    vmem = pltpu.VMEM
    message, plain = 4 * states + 8, 4 * states
    group = like(chips, parts, message, LANES)
    single = like(parts, message, LANES)
    half = like(parts, 2 * states, LANES)
    bare = like(parts, plain, LANES)
    pair = like(chips, parts, plain, LANES)
    made = call(
        functools.partial(states_kernel, chunks, chips, heads, states),
        [group] * (2 * chunks),
        [pl.ANY] * 2 + [vmem],
        300 * 10**6,
        4 * 10**6,
        "states",
        [
            pltpu.VMEM((length, channels), BF16),
            pltpu.VMEM((length, channels), BF16),
            pltpu.SemaphoreType.DMA((2, channels // WIDE)),
        ],
        ROOM,
    )(x, cot, pack)
    keep, send = made[:chunks], made[chunks:]

    def device(plane, chip, core):
        return (plane * chips + chip) * 2 + core

    every = [(p, a, c) for p in range(planes) for a in range(chips) for c in range(2)]
    swap = [(device(p, a, c), device(p, a, 1 - c)) for p, a, c in every]

    def turn(shift):
        return [(device(p, a, c), device(p, (a + shift) % chips, c)) for p, a, c in every]

    def across(level):
        return [(device(p, a, c), device(p ^ 2**level, a, c)) for p, a, c in every]

    def send_to(value, perm):
        return lax.ppermute(value, "seq", perm)

    gots, chipped = [], []
    for k in range(chunks):
        gots.append(send_to(send[k], swap))
        chipped.append(call(functools.partial(chip_kernel, chips), [single] * chips, [vmem] * 2, 10**6, 10**6, "chip")(keep[k], gots[k]))
    size = 4 * parts * states * LANES * 4
    gathered = []
    for k in range(chunks):
        pieces = [chipped[k][0]] + [None] * (chips - 1)
        for shift in range(1, chips):
            pieces[chips - shift] = send_to(chipped[k][shift], turn(shift))
        gathered.append(pieces)
    extra, arrivals, far_states = 1, [], []
    members = math.gcd(MEMBERS, chunks)
    merged = like(members * parts, message, LANES)
    merged_half = like(members * parts, 2 * states, LANES)
    owns, theirs_in = [], []
    for group_start in range(0, chunks, members):
        chunk_range = range(group_start, group_start + members)
        pieces = [piece for k in chunk_range for piece in gathered[k]]
        given = []
        for k in chunk_range:
            onward = call(functools.partial(plane_kernel, chips, 1), single, [vmem] * chips, 10**6, size * 3, "plane")(
                *gathered[k]
            )
            before = []
            for level in range(levels - 2):
                arrived = send_to(onward, across(level))
                step = functools.partial(hop_kernel, chips, 1, level, False)
                entry, onward = call(step, [single] * 2, [vmem] * (2 + len(before)), 10**6, size * 4, "hop")(*before, onward, arrived)
                before = [entry]
            given += [*before, onward, send_to(onward, across(levels - 2))]
        step = functools.partial(hop_kernel, chips, members, levels - 2, True)
        behind = arrivals[-2][:1] if len(arrivals) >= 2 else []
        spaces = [vmem] * len(given) + [pl.ANY] * len(behind)
        entry, onward = call(step, [merged, merged_half], spaces, 10**6, size * 4, "hop")(*given, *behind)
        before = [entry]
        arrived = send_to(onward, across(levels - 1))
        placed = call(
            functools.partial(spread_kernel, chips, members, levels - 1),
            [bare] * (chips * members),
            [vmem] * (2 + chips * members),
            10**6,
            size * 5,
            "spread",
        )(*before, arrived, *pieces)
        for member in range(members):
            mine = placed[member * chips : (member + 1) * chips]
            arrivals.append(mine)
            far_states.append([send_to(mine[shift], turn(shift)) for shift in range(1, chips)])
    inner = call(
        functools.partial(inner_kernel, heads, states),
        [
            like(3 * length, heads),
            like(length, states),
            like(length, states),
            like(channels // WIDE, message, WIDE),
        ],
        [vmem] * 3 + [pl.ANY] * chunks,
        10**9,
        8 * 10**6,
        "inner",
    )(x, cot, pack, *[value[0] for value in arrivals])
    for k in range(chunks):
        mine, theirs = call(
            functools.partial(core_kernel, chips, extra), [pair] * 2, [pl.ANY] + [vmem] * (2 + chips), 10**6, size * 8, "core"
        )(inner[1], keep[k], gots[k], arrivals[k][0], *far_states[k])
        owns.append(mine)
        theirs_in.append(send_to(theirs, swap))

    small = call(
        functools.partial(rates_kernel, chunks, chips), like(2, heads), [vmem] * (1 + 2 * chunks), 10**6, 4 * 10**6, "rates"
    )(inner[3], *owns, *theirs_in)
    count = devices * lax.axis_size("dp")
    copies = jnp.broadcast_to(small[None], (count,) + small.shape)
    total = jnp.sum(lax.all_to_all(copies, ("seq", "dp"), 0, 0, tiled=True), axis=0)
    outputs, grad_inputs, grad_steps, grad_write, grad_read = call(
        functools.partial(finish_kernel, chunks, chips, heads, states),
        [
            like(length, channels, kind=BF16),
            like(length, channels, kind=BF16),
            like(heads, length),
            like(states, length),
            like(states, length),
        ],
        [vmem] * (6 + 2 * chunks),
        2 * 10**9,
        6 * 10**6,
        "finish",
    )(x, cot, pack, *inner[:3], *owns, *theirs_in)
    return (outputs[None], grad_inputs[None], grad_steps.T[None], grad_write.T[None], grad_read.T[None], total[0], total[1])


def solution(mesh):
    along = P("dp", "seq", None)
    chips = 2 ** (int(math.log2(mesh.shape["seq"] // 2)) // 2)
    return jax.shard_map(
        functools.partial(local, chips),
        mesh=mesh,
        in_specs=(along, along, along, along, P(), P(), P("dp", None), along),
        out_specs=(along, along, along, along, along, P(), P()),
        check_vma=False,
    )
```
